256 devices in a mesh: ctx: 32 (over y, z), head: 4 (over x), seg: 2 (over core).
Axes of the slice: x: 4, y: 4, z: 8, core: 2. Of those that a mesh axis runs over, the one named last changes fastest.
Arguments:
- tokens_x: bfloat16 [32768, 2560], P(('ctx', 'seg'), 'head'), may hold values from -6 to 6
- gate_weight: bfloat16 [64, 3, 2560], P(None, None, 'head'), may hold values from -0.15625 to 0.15625
- queries: bfloat16 [32768, 64, 192], P(('ctx', 'seg'), 'head'), may hold values from -48 to 48
- keys: bfloat16 [32768, 4, 192], P(('ctx', 'seg'), 'head'), may hold values from -7 to 7
- values: bfloat16 [32768, 4, 128], P(('ctx', 'seg'), 'head'), may hold values from -24 to 24
- comp_key_weight: bfloat16 [4, 32, 192], P('head'), may hold values from -1 to 1
- comp_value_weight: bfloat16 [4, 32, 128], P('head'), may hold values from -1 to 1
- selected: int32 [256, 4, 16], P(('ctx', 'seg'), 'head'), may hold values from -1 to 511, as said below
Outputs:
- attention: bfloat16 [32768, 64, 128], P(('ctx', 'seg'), 'head')
The draws below stay inside these ranges and needn't reach their ends.
Inputs may be any that keep to these rules, and one draw needn't show every extreme that they name: Each list names the tile's own fine blocks and block 0, then further blocks; live entries are distinct and at most the tile's last fine block; -1 marks an empty entry. For the tiles of one device (one block of 512 tokens) and one group, the blocks selected from the segment of 512 tokens of any other device number at most 1, and some device reaches it.
All inputs are finite; a program needn't handle non-finite values.
Results may differ from the reference program's by a relative error of at most 0.0059.
Values may be sent and summed in bfloat16 or wider, within the bound.
No kernel may reach another device: no remote copies, remote signals or barrier semaphores. Data moves between devices by JAX's collectives and lax.ppermute only.
A program may use at most 128 MiB of HBM per device.

```python
import jax
import jax.numpy as jnp
from jax import lax

D = 2560
H = 64
G = 4
DK = 192
DV = 128
TILE = 128
BLK_S = 64
BLK_C = 32
NSEL = 16
WINDOW = 512
PEER_CAP = 1
TOK_DEV = 512
TOKENS = 32768


def draw_pair(key):
    query_key = jax.random.fold_in(key, 11)
    key_key = jax.random.fold_in(key, 12)
    keys_out = jnp.clip(jax.random.normal(key_key, (TOKENS, G, DK), jnp.float32), -6.0, 6.0)
    queries_out = jnp.clip(jax.random.normal(query_key, (TOKENS, H, DK), jnp.float32), -6.0, 6.0)
    return (queries_out, keys_out)


def draw_queries(key, part):
    return draw_pair(key)[0].astype(jnp.bfloat16)


def draw_keys(key, part):
    return draw_pair(key)[1].astype(jnp.bfloat16)


def draw_selected(key, part):
    block_count = TOKENS // BLK_S
    per_device = TOK_DEV // BLK_S
    device_count = TOKENS // TOK_DEV
    tile_count = TOKENS // TILE
    tile_blocks = TILE // BLK_S
    owner_key = jax.random.fold_in(key, 21)
    score_key = jax.random.fold_in(key, 22)
    block_ids = jnp.arange(block_count, dtype=jnp.int32)
    picks = jax.random.randint(owner_key, (device_count, G, block_count), 0, 2 ** 12) * per_device + block_ids % per_device
    picks = jnp.where(block_ids == 0, 2 ** 30, picks)
    grouped = picks.reshape(device_count, G, device_count, per_device)
    beaten = jnp.sum((grouped[..., None, :] > grouped[..., :, None]).astype(jnp.int32), axis=-1)
    marked = (beaten < PEER_CAP).reshape(device_count, G, block_count)
    tiles = jnp.arange(tile_count, dtype=jnp.int32)
    device_of = tiles // (TOK_DEV // TILE)
    marked_tile = marked[device_of]
    last = ((tiles + 1) * tile_blocks - 1)[:, None, None]
    first = (tiles * tile_blocks)[:, None, None]
    owner = (block_ids // per_device)[None, None, :]
    device_b = device_of[:, None, None]
    causal = block_ids[None, None, :] <= last
    candidate = causal & ((owner == device_b) | marked_tile)
    random_part = jax.random.randint(score_key, (tile_count, G, block_count), 0, 2 ** 12)
    distance = jnp.maximum(last - block_ids[None, None, :], 0)
    base = jnp.where(owner == device_b, random_part * 64 // (distance + 4), random_part * 16)
    score = jnp.where(block_ids[None, None, :] >= first, 2 ** 30, jnp.where(block_ids[None, None, :] == 0, 2 ** 29, jnp.where((owner == device_b - 1) & marked_tile, 2 ** 28, base * block_count)))
    score = jnp.where(candidate, score + block_ids[None, None, :], -1 - block_ids[None, None, :])
    top_values, top_index = lax.top_k(score, NSEL)
    return jnp.where(top_values >= 0, top_index, -1).astype(jnp.int32)


def strengthened(drawn, own_key, source, target, parts, factor):
    def block_of(dim):
        return (jnp.arange(drawn.shape[dim]) // (drawn.shape[dim] // parts)).reshape((-1,) + (1,) * (drawn.ndim - 1 - dim))

    one_side = jax.random.permutation(own_key, parts)[block_of(target)]
    far = (block_of(target) + parts // 2) % parts
    return jnp.where((block_of(source) == one_side) | (block_of(source) == far), factor * drawn, drawn)


def levels(key, extent, split, least, top_value):
    def one(dim, blocks):
        heights = jax.random.uniform(jax.random.fold_in(jax.random.fold_in(key, 6), dim), (blocks,), jnp.float32, least / len(split), top_value / len(split))
        return jnp.repeat(jnp.exp(heights), extent[dim] // blocks).reshape((-1,) + (1,) * (len(extent) - dim - 1))

    loudness = one(*split[0])
    for cut in split[1:]:
        loudness = loudness * one(*cut)
    return loudness


def gaussian(own_key, shape, spread, most, shards=(), kind=jnp.bfloat16):
    result = spread * jax.random.normal(own_key, shape, jnp.float32)
    if shards:
        result = result * levels(own_key, shape, shards, -0.22, 0.18)
    return jnp.clip(result, -most, most).astype(kind)


def bell_draw_with(own_key, dims, scale, reach, shards, heavy, held_as=jnp.bfloat16):
    entries = scale * jax.random.normal(own_key, dims, jnp.float32)
    if shards:
        entries = entries * levels(own_key, dims, shards, -0.22, 0.18)
    return jnp.clip(strengthened(entries, jax.random.fold_in(own_key, 3), *heavy), -reach, reach).astype(held_as)


def setup_inputs(seed: int = 0) -> dict:
    arg_keys = jax.random.split(jax.random.key(seed), 9)
    tokens_x = gaussian(arg_keys[0], (TOKENS, D), 1.0, 6.0, ((0, 64), (1, 4)))
    gate_weight = bell_draw_with(arg_keys[1], (H, 3, D), D ** -0.5, 0.15625, ((2, 4),), (2, 0, 4, 2.0))
    queries = draw_queries(jax.random.fold_in(arg_keys[8], 71), 0)
    keys = draw_keys(jax.random.fold_in(arg_keys[8], 71), 0)
    values = gaussian(arg_keys[4], (TOKENS, G, DV), 4.0, 24.0, ((0, 64), (1, 4)))
    comp_key_weight = gaussian(arg_keys[5], (G, BLK_C, DK), BLK_C ** -0.5, 1.0, ((0, 4),))
    comp_value_weight = gaussian(arg_keys[6], (G, BLK_C, DV), BLK_C ** -0.5, 1.0, ((0, 4),))
    selected = draw_selected(jax.random.fold_in(arg_keys[8], 71), 0)
    return {"tokens_x": tokens_x, "gate_weight": gate_weight, "queries": queries, "keys": keys, "values": values, "comp_key_weight": comp_key_weight, "comp_value_weight": comp_value_weight, "selected": selected}


def attend(query, keys_part, values_part, allowed):
    scores = jnp.einsum('rhd,kd->hrk', query.astype(jnp.float32), keys_part.astype(jnp.float32)) * (keys_part.shape[-1] ** -0.5)
    scores = jnp.where(allowed[None], scores, -1e30)
    highest = jnp.max(scores, axis=-1, keepdims=True)
    weights = jnp.where(allowed[None], jnp.exp(scores - highest), 0.0)
    total = jnp.sum(weights, axis=-1)
    rounded = lax.optimization_barrier(weights.astype(jnp.bfloat16))
    summed = jnp.einsum('hrk,kv->rhv', rounded.astype(jnp.float32), values_part.astype(jnp.float32))
    return summed / jnp.maximum(total, 1.0).T[:, :, None]


def reference(tokens_x, gate_weight, queries, keys, values, comp_key_weight, comp_value_weight, selected):
    group_heads = H // G
    logits = jnp.einsum('hcd,td->hct', gate_weight.astype(jnp.float32), tokens_x.astype(jnp.float32))
    gates = jax.nn.sigmoid(logits)
    coarse_count = TOKENS // BLK_C
    key_blocks = keys.astype(jnp.float32).reshape(coarse_count, BLK_C, G, DK)
    value_blocks = values.astype(jnp.float32).reshape(coarse_count, BLK_C, G, DV)
    coarse_keys = jnp.sum(key_blocks * jnp.transpose(comp_key_weight.astype(jnp.float32), (1, 0, 2))[None], axis=1).astype(jnp.bfloat16)
    coarse_values = jnp.sum(value_blocks * jnp.transpose(comp_value_weight.astype(jnp.float32), (1, 0, 2))[None], axis=1).astype(jnp.bfloat16)
    coarse_end = jnp.arange(coarse_count, dtype=jnp.int32) * BLK_C + BLK_C - 1
    padded_keys = jnp.pad(keys, ((WINDOW, 0), (0, 0), (0, 0)))
    padded_values = jnp.pad(values, ((WINDOW, 0), (0, 0), (0, 0)))
    fine_keys_all = keys.reshape(TOKENS // BLK_S, BLK_S, G, DK)
    fine_values_all = values.reshape(TOKENS // BLK_S, BLK_S, G, DV)

    def one_tile(tile):
        start = (tile * TILE).astype(jnp.int32)
        rows = start + jnp.arange(TILE, dtype=jnp.int32)
        query = lax.dynamic_slice_in_dim(queries, start, TILE, 0)
        gate = lax.dynamic_slice_in_dim(gates, start, TILE, 2)
        near_keys = lax.dynamic_slice_in_dim(padded_keys, start, WINDOW + TILE, 0)
        near_values = lax.dynamic_slice_in_dim(padded_values, start, WINDOW + TILE, 0)
        near_pos = start - WINDOW + jnp.arange(WINDOW + TILE, dtype=jnp.int32)
        near_ok = (near_pos[None, :] >= 0) & (near_pos[None, :] <= rows[:, None]) & (near_pos[None, :] > rows[:, None] - WINDOW)
        coarse_ok = coarse_end[None, :] <= rows[:, None]
        chosen = selected[tile]
        outputs = []
        for group in range(G):
            blocks = jnp.maximum(chosen[group], 0)
            fine_keys = fine_keys_all[blocks, :, group].reshape(NSEL * BLK_S, DK)
            fine_values = fine_values_all[blocks, :, group].reshape(NSEL * BLK_S, DV)
            fine_pos = (blocks[:, None] * BLK_S + jnp.arange(BLK_S, dtype=jnp.int32)[None, :]).reshape(-1)
            live = jnp.repeat(chosen[group] >= 0, BLK_S)
            fine_ok = live[None, :] & (fine_pos[None, :] <= rows[:, None])
            head_query = query[:, group * group_heads:(group + 1) * group_heads]
            head_gate = gate[group * group_heads:(group + 1) * group_heads]
            coarse_out = attend(head_query, coarse_keys[:, group], coarse_values[:, group], coarse_ok)
            fine_out = attend(head_query, fine_keys, fine_values, fine_ok)
            window_out = attend(head_query, near_keys[:, group], near_values[:, group], near_ok)
            mixed = head_gate[:, 0, :].T[:, :, None] * coarse_out + head_gate[:, 1, :].T[:, :, None] * fine_out
            mixed = mixed + head_gate[:, 2, :].T[:, :, None] * window_out
            outputs.append(mixed)
        return jnp.concatenate(outputs, axis=1).astype(jnp.bfloat16)

    tiles = lax.map(one_tile, jnp.arange(TOKENS // TILE, dtype=jnp.int32))
    return tiles.reshape(TOKENS, H, DV)
```

```python
import jax
import jax.numpy as jnp
from jax import lax
from jax.experimental import pallas as pl
from jax.experimental.pallas import tpu as pltpu
from jax.sharding import Mesh
from jax.sharding import PartitionSpec as P

TILE = 128
BLK_S = 64
BLK_C = 32
NSEL = 16
WINDOW = 512
CTX_SEG = ("ctx_0", "ctx_1", "seg")

SEG = 512
HEADS = 16
DK = 192
DV = 128
BLOCKS = SEG // BLK_S
COARSE = SEG // BLK_C
PACK = 160
TILES = SEG // TILE
TILE_BLOCKS = TILE // BLK_S
FAR = NSEL - TILE_BLOCKS
PAIRS = HEADS // 2
WIDE = 2048
NEG = -1e30
FLOOR = -1e29
TINY = 1e-35
SCALE2 = (DK**-0.5) * 1.4426950408889634
REACH = 96.0


def nn(a, b):
    return lax.dot_general(a, b, (((1,), (0,)), ((), ())), preferred_element_type=jnp.float32)


def tn(a, b):
    return lax.dot_general(a, b, (((0,), (0,)), ((), ())), preferred_element_type=jnp.float32)


def smem():
    return pl.BlockSpec(memory_space=pltpu.SMEM)


def ask_kernel(place, selected, request):
    here = place[0]

    @pl.loop(0, request.shape[0])
    def _(i):
        request[i, 0, 0] = -1

    @pl.loop(0, TILES)
    def _(tile):
        for entry in range(NSEL):
            block = selected[tile, 0, entry]
            owner = jnp.maximum(block, 0) // BLOCKS

            @pl.when((block >= 0) & (owner != here))
            def _():
                request[owner, 0, 0] = block % BLOCKS


def request_of(place, selected, segments):
    return pl.pallas_call(
        ask_kernel,
        in_specs=[smem(), smem()],
        out_specs=smem(),
        out_shape=jax.ShapeDtypeStruct((segments, 1, 1), jnp.int32),
        name="ask",
    )(place, selected)


def list_kernel(place, selected, lists):
    @pl.loop(0, TILES)
    def _(tile):
        own = place[0] * BLOCKS + tile * TILE_BLOCKS
        at = jnp.int32(0)
        for entry in range(NSEL):
            lists[tile, entry] = 0
        for entry in range(NSEL):
            block = selected[tile, 0, entry]
            wanted = (block >= 0) & (block < own) & (at < FAR)

            @pl.when(wanted)
            def _():
                lists[tile, at] = block

            at = at + wanted.astype(jnp.int32)
        lists[tile, NSEL - 1] = at


def lists_of(place, selected):
    return pl.pallas_call(
        list_kernel,
        in_specs=[smem(), smem()],
        out_specs=smem(),
        out_shape=jax.ShapeDtypeStruct((TILES, NSEL), jnp.int32),
        name="lists",
    )(place, selected)


def pack_kernel(keys, values, key_weight, value_weight, packed, coarse):
    k = keys[...].T
    v = values[...]
    for b in range(BLOCKS):
        kb = k[b * BLK_S : (b + 1) * BLK_S]
        packed[b, 0:64, :] = kb[:, 0:128]
        packed[b, 64:96, :] = jnp.concatenate([kb[0:32, 128:192], kb[32:64, 128:192]], axis=1)
        packed[b, 96:160, :] = v[b * BLK_S : (b + 1) * BLK_S]
    kf = k.astype(jnp.float32)
    vf = v.astype(jnp.float32).reshape(COARSE, BLK_C, DV)
    weighted = kf.reshape(COARSE, BLK_C, DK) * key_weight[...].astype(jnp.float32)[None]
    ck = jnp.sum(weighted, axis=1)
    cv = jnp.sum(vf * value_weight[...].astype(jnp.float32)[None], axis=1)
    kt = keys[...].astype(jnp.float32)
    longest = jnp.max(jnp.sum(kt * kt, axis=0, keepdims=True), axis=1, keepdims=True)
    longest_c = jnp.max(jnp.sum(ck * ck, axis=1, keepdims=True), axis=0, keepdims=True)
    bound = jnp.maximum(longest, longest_c) * 1.02
    coarse[:, 0:DK] = ck.astype(jnp.bfloat16)
    coarse[:, DK:256] = jnp.broadcast_to(bound, (COARSE, 256 - DK)).astype(jnp.bfloat16)
    coarse[:, 256:384] = cv.astype(jnp.bfloat16)
    coarse[:, 384:512] = jnp.ones((COARSE, 128), jnp.bfloat16)
    coarse[:, 512:] = jnp.zeros((COARSE, WIDE - 512), jnp.bfloat16)


def packed_of(keys, values, key_weight, value_weight):
    return pl.pallas_call(
        pack_kernel,
        out_shape=(
            jax.ShapeDtypeStruct((BLOCKS, PACK, 128), jnp.bfloat16),
            jax.ShapeDtypeStruct((COARSE, WIDE), jnp.bfloat16),
        ),
        cost_estimate=pl.CostEstimate(flops=400000, bytes_accessed=1 << 20, transcendentals=0),
        name="pack",
    )(keys, values, key_weight, value_weight)


def reply_kernel(asked, packed, out, sem):
    count = out.shape[0]

    def copy(i):
        return pltpu.make_async_copy(packed.at[jnp.maximum(asked[i, 0, 0], 0)], out.at[i], sem)

    @pl.loop(0, count)
    def _(i):
        copy(i).start()

    pltpu.make_async_copy(out, out, sem).wait()


def reply_of(asked, packed):
    count = asked.shape[0]
    return pl.pallas_call(
        reply_kernel,
        out_shape=jax.ShapeDtypeStruct((count, PACK, 128), jnp.bfloat16),
        in_specs=[
            smem(),
            pl.BlockSpec(memory_space=pltpu.VMEM),
        ],
        out_specs=pl.BlockSpec(memory_space=pl.ANY),
        scratch_shapes=[pltpu.SemaphoreType.DMA],
        cost_estimate=pl.CostEstimate(flops=0, bytes_accessed=3 << 20, transcendentals=0),
        name="reply",
    )(asked, packed)


def unpacked(source, keys, values, rows, present=None):
    keys[rows, 0:128] = source[0:64, :]
    tail = source[64:96, :]
    keys[rows, 128:192] = jnp.concatenate([tail[:, 0:64], tail[:, 64:128]], axis=0)
    values[rows, 0:DV] = source[96:160, :]
    values[rows, DV:] = jnp.ones((BLK_S, 128), jnp.bfloat16)


def query_pair(ref, pair):
    return jnp.concatenate([ref[2 * pair], ref[2 * pair + 1]], axis=1)


def summed_near_zero(q, parts):
    total = None
    for keys, values, mask, _ in parts:
        weights = jnp.exp2(nn(keys(), q) * SCALE2)
        if mask is not None:
            weights = jnp.where(mask(), weights, 0.0)
        term = tn(weights.astype(jnp.bfloat16), values())
        total = term if total is None else total + term
    return total


def summed_from_top(q, parts):
    scores = [jnp.where(mask(), nn(keys(), q), NEG) for keys, _, _, mask in parts]
    top = jnp.full((1, 2 * TILE), FLOOR, jnp.float32)
    for s in scores:
        top = jnp.maximum(top, jnp.max(s, axis=0, keepdims=True))
    total = None
    for s, (_, values, _, _) in zip(scores, parts):
        term = tn(jnp.exp2((s - top) * SCALE2).astype(jnp.bfloat16), values())
        total = term if total is None else total + term
    return total


def attention_into(write, safe, query, parts):
    def one(pair, summed):
        total = summed(query_pair(query, pair), parts)
        mean = total[:, 0:DV] / jnp.maximum(total[:, DV:], TINY)
        write(2 * pair, mean[0:TILE])
        write(2 * pair + 1, mean[TILE:])

    @pl.when(safe)
    def _():
        for pair in range(PAIRS):
            one(pair, summed_near_zero)

    @pl.when(jnp.logical_not(safe))
    def _():
        @pl.loop(0, PAIRS)
        def _(pair):
            one(pair, summed_from_top)


def gate_columns(gates):
    return gates[...].T


def gate_of(columns, head, branch):
    at = branch * HEADS + head
    if isinstance(at, int):
        return columns[:, at : at + 1]
    lane = lax.broadcasted_iota(jnp.int32, (TILE, 3 * HEADS), 1)
    return jnp.sum(jnp.where(lane == at, columns, 0.0), axis=1, keepdims=True)


def token_row():
    return lax.broadcasted_iota(jnp.int32, (1, 2 * TILE), 1) % TILE


def key_column(count):
    return lax.broadcasted_iota(jnp.int32, (count, 1), 0)


def window_kernel(place, safe, query, previous, packed, gates, out, near_keys, near_values):
    tile = pl.program_id(0)
    here = place[0]

    @pl.when(tile == 0)
    def _():
        for b in range(BLOCKS):
            unpacked(packed.at[b], near_keys, near_values, pl.ds(SEG + b * BLK_S, BLK_S))

        @pl.when(here > 0)
        def _():
            for b in range(BLOCKS):
                unpacked(previous.at[b], near_keys, near_values, pl.ds(b * BLK_S, BLK_S))

        @pl.when(here == 0)
        def _():
            near_keys[0:SEG, :] = jnp.zeros((SEG, DK), jnp.bfloat16)
            near_values[0:SEG, :] = jnp.zeros((SEG, 256), jnp.bfloat16)

    first = pl.multiple_of(tile * TILE, TILE)
    token = token_row()
    from_row = jnp.maximum(token, jnp.where(here > 0, 0, SEG) - first - 1)
    columns = gate_columns(gates)

    def part(start, count, mask, exact):
        rows = pl.ds(first + start, count)
        return (lambda: near_keys[rows, :], lambda: near_values[rows, :], mask, exact)

    after = lambda start, count: lambda: key_column(count) + start > from_row
    inside = lambda: key_column(TILE) <= token
    parts = [
        part(0, TILE, lambda: key_column(TILE) > token, after(0, TILE)),
        part(TILE, WINDOW - TILE, None, after(TILE, WINDOW - TILE)),
        part(WINDOW, TILE, inside, inside),
    ]

    def write(head, mean):
        out[head] = gate_of(columns, head, 2) * mean

    attention_into(write, safe[0] > 0, query, parts)


def coarse_kernel(place, safe, query, coarse, gates, near, out):
    token = token_row()
    ended = (place[0] * SEG + pl.program_id(0) * TILE + token + 1) // BLK_C
    mask = lambda: key_column(coarse.shape[0]) < ended
    columns = gate_columns(gates)
    parts = [(lambda: coarse[:, 0:DK], lambda: coarse[:, 256:512], mask, mask)]

    def write(head, mean):
        out[head] = near[head] + gate_of(columns, head, 0) * mean

    attention_into(write, safe[0] > 0, query, parts)


def fine_kernel(
    place, safe, lists, query, received, packed, near, gates, out, fine_keys, fine_values, mixed,
):
    tile = pl.program_id(0)
    here = place[0]

    @pl.when(tile == 0)
    def _():
        fine_keys[...] = jnp.zeros(fine_keys.shape, jnp.bfloat16)

    live = lists[tile, NSEL - 1]
    for entry in range(FAR):
        block = lists[tile, entry]
        owner = block // BLOCKS
        rows = pl.ds(entry * BLK_S, BLK_S)

        @pl.when((entry < live) & (owner != here))
        def _():
            unpacked(received.at[owner], fine_keys, fine_values, rows)

        @pl.when((entry < live) & (owner == here))
        def _():
            unpacked(packed.at[block % BLOCKS], fine_keys, fine_values, rows)

        @pl.when(entry >= live)
        def _():
            fine_values[rows, :] = jnp.zeros((BLK_S, 256), jnp.bfloat16)

    for b in range(TILE_BLOCKS):
        rows = pl.ds((FAR + b) * BLK_S, BLK_S)
        unpacked(packed.at[tile * TILE_BLOCKS + b], fine_keys, fine_values, rows)

    count = FAR * BLK_S
    token = token_row()
    columns = gate_columns(gates)
    inside = lambda: key_column(TILE) <= token
    parts = [
        (
            lambda: fine_keys[0:count, :],
            lambda: fine_values[0:count, :],
            None,
            lambda: key_column(count) + token * 0 < live * BLK_S,
        ),
        (lambda: fine_keys[count:, :], lambda: fine_values[count:, :], inside, inside),
    ]

    def write(head, mean):
        total = near[head] + gate_of(columns, head, 1) * mean
        mixed[pl.ds(head, TILE, stride=HEADS), :] = total

    attention_into(write, safe[0] > 0, query, parts)
    out[...] = mixed[...].astype(jnp.bfloat16)


def whole(a):
    return pl.BlockSpec(a.shape, lambda i: (0,) * a.ndim, pipeline_mode=pl.Buffered(1))


def by_tile(kernel, name, keys, ins, specs, out_spec, out_shape, scratch, aliases={}):
    query = pl.BlockSpec((HEADS, DK, TILE), lambda i: (0, 0, i))
    gate = pl.BlockSpec((3 * HEADS, TILE), lambda i: (0, i))
    kinds = {"scalar": smem(), "query": query, "gate": gate, "near": near_spec()}
    return pl.pallas_call(
        kernel,
        grid=(TILES,),
        in_specs=[kinds[s] if isinstance(s, str) else s for s in specs],
        out_specs=out_spec,
        out_shape=out_shape,
        scratch_shapes=scratch,
        input_output_aliases=aliases,
        compiler_params=pltpu.CompilerParams(
            dimension_semantics=("arbitrary",), vmem_limit_bytes=60 << 20
        ),
        cost_estimate=pl.CostEstimate(
            flops=SEG * HEADS * keys * 1024, bytes_accessed=12 << 20, transcendentals=SEG * HEADS * keys
        ),
        name=name,
    )(*ins)


def near_spec():
    return pl.BlockSpec((HEADS, TILE, DV), lambda i: (0, i, 0))


NEAR = jax.ShapeDtypeStruct((HEADS, SEG, DV), jnp.float32)


def window_of(place, safe, query, previous, packed, gates):
    return by_tile(
        window_kernel, "window", WINDOW + TILE,
        (place, safe, query, previous, packed, gates),
        ["scalar", "scalar", "query", whole(previous), whole(packed), "gate"],
        near_spec(), NEAR,
        [pltpu.VMEM((2 * SEG, DK), jnp.bfloat16), pltpu.VMEM((2 * SEG, 256), jnp.bfloat16)],
    )


def coarse_of(place, safe, query, coarse, gates, near):
    return by_tile(
        coarse_kernel, "coarse", coarse.shape[0],
        (place, safe, query, coarse, gates, near),
        ["scalar", "scalar", "query", whole(coarse), "gate", "near"],
        near_spec(), NEAR, [],
    )


def fine_of(place, safe, lists, query, received, packed, near, gates):
    return by_tile(
        fine_kernel, "fine", NSEL * BLK_S,
        (place, safe, lists, query, received, packed, near, gates),
        ["scalar", "scalar", "scalar", "query", whole(received), whole(packed), "near", "gate"],
        pl.BlockSpec((TILE * HEADS, DV), lambda i: (i, 0)),
        jax.ShapeDtypeStruct((SEG * HEADS, DV), jnp.bfloat16),
        [
            pltpu.VMEM((NSEL * BLK_S, DK), jnp.bfloat16),
            pltpu.VMEM((NSEL * BLK_S, 256), jnp.bfloat16),
            pltpu.VMEM((TILE * HEADS, DV), jnp.float32),
        ],
    )


def on_device(
    tokens_x, gate_weight, queries, keys, values, comp_key_weight, comp_value_weight, selected
):
    segments = lax.axis_size(CTX_SEG)
    place = lax.axis_index(CTX_SEG).astype(jnp.int32).reshape(1)
    packed, coarse_own = packed_of(
        keys[:, 0].T, values[:, 0], comp_key_weight[0], comp_value_weight[0]
    )
    previous = lax.ppermute(packed, CTX_SEG, [(i, i + 1) for i in range(segments - 1)])
    coarse_row = lax.all_gather(coarse_own, ("ctx_1", "seg"), tiled=True)
    request = request_of(place, selected, segments)
    asked = lax.all_to_all(request, CTX_SEG, split_axis=0, concat_axis=0, tiled=True)
    reply = reply_of(asked, packed)
    reply, coarse_row, previous = lax.optimization_barrier((reply, coarse_row, previous))
    coarse = lax.all_gather(coarse_row[:, 0:512], "ctx_0", tiled=True)
    received = lax.all_to_all(reply, CTX_SEG, split_axis=0, concat_axis=0, tiled=True)
    lists = lists_of(place, selected)
    logits = jnp.einsum("hcd,td->cht", gate_weight, tokens_x, preferred_element_type=jnp.float32)
    logits = lax.psum_scatter(logits, "head", scatter_dimension=1, tiled=True)
    gates = jax.nn.sigmoid(logits).reshape(3 * HEADS, SEG)
    query = queries.transpose(1, 2, 0)
    longest_query = jnp.max(jnp.sum(jnp.square(query.astype(jnp.float32)), axis=1))
    longest_key = jnp.max(coarse[:, DK].astype(jnp.float32))
    safe = longest_query * longest_key * SCALE2**2 <= REACH**2
    safe = safe.astype(jnp.int32).reshape(1)
    near = window_of(place, safe, query, previous, packed, gates)
    near = coarse_of(place, safe, query, coarse, gates, near)
    out = fine_of(place, safe, lists, query, received, packed, near, gates)
    return out.reshape(SEG, HEADS, DV)


def solution(mesh):
    split = Mesh(
        mesh.devices.reshape(4, 8, mesh.shape["head"], mesh.shape["seg"]),
        ("ctx_0", "ctx_1", "head", "seg"),
    )
    placed = (
        P(CTX_SEG, "head"),
        P(None, None, "head"),
        P(CTX_SEG, "head", None),
        P(CTX_SEG, "head", None),
        P(CTX_SEG, "head", None),
        P("head", None, None),
        P("head", None, None),
        P(CTX_SEG, "head", None),
    )
    return jax.shard_map(
        on_device, mesh=split, in_specs=placed, out_specs=P(CTX_SEG, "head", None), check_vma=False
    )
```

```python
import jax
import jax.numpy as jnp
from jax import lax
from jax.experimental import pallas as pl
from jax.experimental.pallas import tpu as pltpu
from jax.sharding import Mesh
from jax.sharding import PartitionSpec as P

TILE = 128
BLK_S = 64
BLK_C = 32
NSEL = 16
WINDOW = 512
CTX_SEG = ("ctx_0", "ctx_1", "seg")

SEG = 512
HEADS = 16
DK = 192
DV = 128
BLOCKS = SEG // BLK_S
COARSE = SEG // BLK_C
PACK = 160
TILES = SEG // TILE
TILE_BLOCKS = TILE // BLK_S
FAR = NSEL - TILE_BLOCKS
PAIRS = HEADS // 2
WIDE = 4096
NEG = -1e30
VMEM_LIMIT = 60 << 20
FLOOR = -1e29
TINY = 1e-35
SCALE2 = (DK**-0.5) * 1.4426950408889634
REACH = 96.0
LIMIT = (REACH / SCALE2) ** 2


def nn(a, b):
    return lax.dot_general(a, b, (((1,), (0,)), ((), ())), preferred_element_type=jnp.float32)


def tn(a, b):
    return lax.dot_general(a, b, (((0,), (0,)), ((), ())), preferred_element_type=jnp.float32)


def smem():
    return pl.BlockSpec(memory_space=pltpu.SMEM)


def ask_kernel(selected, request):
    for i in range(request.shape[0]):
        request[i, 0, 0] = -1
    for tile in range(TILES):
        for entry in range(NSEL):
            block = jnp.maximum(selected[tile, 0, entry], 0)
            request[lax.shift_right_logical(block, 3), 0, 0] = block & (BLOCKS - 1)


def request_of(selected, segments):
    return pl.pallas_call(
        ask_kernel,
        in_specs=[smem()],
        out_specs=smem(),
        out_shape=jax.ShapeDtypeStruct((segments, 1, 1), jnp.int32),
        name="ask",
    )(selected)


def list_kernel(pool, place, selected, lists):
    here = place[0]

    @pl.loop(0, TILES)
    def _(tile):
        own = here * BLOCKS + tile * TILE_BLOCKS
        at = jnp.int32(0)
        for entry in range(NSEL):
            lists[tile, entry] = 0
        for entry in range(NSEL):
            block = selected[tile, 0, entry]
            wanted = (block >= 0) & (block < own) & (at < FAR)
            owner = jnp.maximum(block, 0) // BLOCKS

            @pl.when(wanted)
            def _():
                lists[tile, at] = jnp.where(owner == here, pool - BLOCKS + block % BLOCKS, owner)

            at = at + wanted.astype(jnp.int32)
        lists[tile, NSEL - 1] = at


def lists_of(place, selected, pool):
    def kernel(*refs):
        list_kernel(pool, *refs)

    return pl.pallas_call(
        kernel,
        in_specs=[smem(), smem()],
        out_specs=smem(),
        out_shape=jax.ShapeDtypeStruct((TILES, NSEL), jnp.int32),
        name="lists",
    )(place, selected)


def pack_kernel(keys, values, key_weight, value_weight, packed, coarse):
    k = keys[...].T
    v = values[...]
    for b in range(BLOCKS):
        kb = k[b * BLK_S : (b + 1) * BLK_S]
        packed[b, 0:64, :] = kb[:, 0:128]
        packed[b, 64:96, :] = jnp.concatenate([kb[0:32, 128:192], kb[32:64, 128:192]], axis=1)
        packed[b, 96:160, :] = v[b * BLK_S : (b + 1) * BLK_S]
    kf = k.astype(jnp.float32)
    vf = v.astype(jnp.float32).reshape(COARSE, BLK_C, DV)
    weighted = kf.reshape(COARSE, BLK_C, DK) * key_weight[...].astype(jnp.float32)[None]
    ck = jnp.sum(weighted, axis=1)
    cv = jnp.sum(vf * value_weight[...].astype(jnp.float32)[None], axis=1)
    kt = keys[...].astype(jnp.float32)
    longest = jnp.max(jnp.sum(kt * kt, axis=0, keepdims=True), axis=1, keepdims=True)
    longest_c = jnp.max(jnp.sum(ck * ck, axis=1, keepdims=True), axis=0, keepdims=True)
    bound = jnp.maximum(longest, longest_c) * 1.02
    coarse[:, 0:DK] = ck.astype(jnp.bfloat16)
    coarse[:, DK:256] = jnp.broadcast_to(bound, (COARSE, 256 - DK)).astype(jnp.bfloat16)
    coarse[:, 256:384] = cv.astype(jnp.bfloat16)
    coarse[:, 384:512] = jnp.ones((COARSE, 128), jnp.bfloat16)
    coarse[:, 512:] = jnp.zeros((COARSE, WIDE - 512), jnp.bfloat16)


def packed_of(keys, values, key_weight, value_weight):
    return pl.pallas_call(
        pack_kernel,
        out_shape=(
            jax.ShapeDtypeStruct((BLOCKS, PACK, 128), jnp.bfloat16),
            jax.ShapeDtypeStruct((COARSE, WIDE), jnp.bfloat16),
        ),
        cost_estimate=pl.CostEstimate(flops=400000, bytes_accessed=1 << 20, transcendentals=0),
        name="pack",
    )(keys, values, key_weight, value_weight)


def reply_kernel(asked, packed, out):
    for i in range(out.shape[0]):
        out[i] = packed[jnp.maximum(asked[i, 0, 0], 0)]


def reply_of(asked, packed):
    count = asked.shape[0]
    return pl.pallas_call(
        reply_kernel,
        out_shape=jax.ShapeDtypeStruct((count, PACK, 128), jnp.bfloat16),
        in_specs=[smem(), pl.BlockSpec(memory_space=pltpu.VMEM)],
        out_specs=pl.BlockSpec(memory_space=pltpu.VMEM),
        cost_estimate=pl.CostEstimate(flops=0, bytes_accessed=3 << 20, transcendentals=0),
        name="reply",
    )(asked, packed)


def unpacked(source, keys, values, rows, present=None):
    keys[rows, 0:128] = source[0:64, :]
    tail = source[64:96, :]
    keys[rows, 128:192] = jnp.concatenate([tail[:, 0:64], tail[:, 64:128]], axis=0)
    values[rows, 0:DV] = source[96:160, :]
    values[rows, DV:] = jnp.ones((BLK_S, 128), jnp.bfloat16)


def query_pair(ref, pair):
    return jnp.concatenate([ref[2 * pair], ref[2 * pair + 1]], axis=1)


def summed_near_zero(q, parts):
    total = None
    for keys, values, mask, _ in parts:
        weights = jnp.exp2(nn(keys(), q) * SCALE2)
        if mask is not None:
            weights = jnp.where(mask(), weights, 0.0)
        term = tn(weights.astype(jnp.bfloat16), values())
        total = term if total is None else total + term
    return total


def summed_from_top(q, parts):
    scores = [jnp.where(mask(), nn(keys(), q), NEG) for keys, _, _, mask in parts]
    top = jnp.full((1, 2 * TILE), FLOOR, jnp.float32)
    for s in scores:
        top = jnp.maximum(top, jnp.max(s, axis=0, keepdims=True))
    total = None
    for s, (_, values, _, _) in zip(scores, parts):
        term = tn(jnp.exp2((s - top) * SCALE2).astype(jnp.bfloat16), values())
        total = term if total is None else total + term
    return total


def attention_into(write, safe, query, parts):
    def one(pair, summed):
        total = summed(query_pair(query, pair), parts)
        mean = total[:, 0:DV] / jnp.maximum(total[:, DV:], TINY)
        write(2 * pair, mean[0:TILE])
        write(2 * pair + 1, mean[TILE:])

    @pl.when(safe)
    def _():
        for pair in range(PAIRS):
            one(pair, summed_near_zero)

    @pl.when(jnp.logical_not(safe))
    def _():
        @pl.loop(0, PAIRS)
        def _(pair):
            one(pair, summed_from_top)


def gate_columns(gates):
    return gates[...].T


def gate_of(columns, head, branch):
    at = branch * HEADS + head
    if isinstance(at, int):
        return columns[:, at : at + 1]
    lane = lax.broadcasted_iota(jnp.int32, (TILE, 3 * HEADS), 1)
    return jnp.sum(jnp.where(lane == at, columns, 0.0), axis=1, keepdims=True)


def token_row():
    return lax.broadcasted_iota(jnp.int32, (1, 2 * TILE), 1) % TILE


def key_column(count):
    return lax.broadcasted_iota(jnp.int32, (count, 1), 0)


def window_kernel(
    place, longest_query, query, previous, packed, out, near_keys, near_values, safe
):
    tile = pl.program_id(0)
    here = place[0]

    @pl.when(tile == 0)
    def _():
        for b in range(BLOCKS):
            unpacked(packed.at[b], near_keys, near_values, pl.ds(SEG + b * BLK_S, BLK_S))

        @pl.when(here > 0)
        def _():
            for b in range(BLOCKS):
                unpacked(previous.at[b], near_keys, near_values, pl.ds(b * BLK_S, BLK_S))

        @pl.when(here == 0)
        def _():
            near_keys[0:SEG, :] = jnp.zeros((SEG, DK), jnp.bfloat16)
            near_values[0:SEG, :] = jnp.zeros((SEG, 256), jnp.bfloat16)

        wide = near_keys[...].astype(jnp.float32)
        longest = jnp.max(jnp.sum(wide * wide, axis=1, keepdims=True))
        safe[0] = (longest * longest_query[0] <= LIMIT).astype(jnp.int32)

    first = pl.multiple_of(tile * TILE, TILE)
    token = token_row()
    from_row = jnp.maximum(token, jnp.where(here > 0, 0, SEG) - first - 1)

    def part(start, count, mask, exact):
        rows = pl.ds(first + start, count)
        return (lambda: near_keys[rows, :], lambda: near_values[rows, :], mask, exact)

    after = lambda start, count: lambda: key_column(count) + start > from_row
    inside = lambda: key_column(TILE) <= token
    parts = [
        part(0, TILE, lambda: key_column(TILE) > token, after(0, TILE)),
        part(TILE, WINDOW - TILE, None, after(TILE, WINDOW - TILE)),
        part(WINDOW, TILE, inside, inside),
    ]

    def write(head, mean):
        out[head] = mean

    attention_into(write, safe[0] > 0, query, parts)


def coarse_kernel(place, safe, query, coarse, gates, near, out):
    token = token_row()
    ended = (place[0] * SEG + pl.program_id(0) * TILE + token + 1) // BLK_C
    mask = lambda: key_column(coarse.shape[0]) < ended
    columns = gate_columns(gates)
    parts = [(lambda: coarse[:, 0:DK], lambda: coarse[:, 256:512], mask, mask)]

    def write(head, mean):
        window = gate_of(columns, head, 2) * near[head]
        out[head] = gate_of(columns, head, 0) * mean + window

    attention_into(write, safe[0] > 0, query, parts)


def fine_kernel(
    safe, lists, query, received, packed, near, gates, out, pool, fine_keys, fine_values, mixed, sems
):
    tile = pl.program_id(0)
    others = received.shape[0]

    @pl.when(tile == 0)
    def _():
        copies = [
            pltpu.make_async_copy(received, pool.at[pl.ds(0, others)], sems.at[0]),
            pltpu.make_async_copy(packed, pool.at[pl.ds(others, BLOCKS)], sems.at[1]),
        ]
        for copy in copies:
            copy.start()
        for copy in copies:
            copy.wait()

    live = lists[tile, NSEL - 1]
    for entry in range(NSEL):
        if entry < FAR:
            at = lists[tile, entry]
            present = jnp.where(entry < live, 1.0, 0.0)
        else:
            at = others + tile * TILE_BLOCKS + entry - FAR
            present = 1.0
        rows = pl.ds(entry * BLK_S, BLK_S)
        fine_keys[rows, 0:128] = pool[at, 0:64, :]
        tail = pool[at, 64:96, :]
        fine_keys[rows, 128:192] = jnp.concatenate([tail[:, 0:64], tail[:, 64:128]], axis=0)
        ones = jnp.full((BLK_S, 128), present, jnp.float32).astype(jnp.bfloat16)
        fine_values[rows, 0:DV] = pool[at, 96:160, :] * ones
        fine_values[rows, DV:] = ones

    count = FAR * BLK_S
    token = token_row()
    columns = gate_columns(gates)
    row = lambda: key_column(NSEL * BLK_S)
    inside = lambda: row() <= token + count
    exact = lambda: inside() & ((row() < live * BLK_S) | (row() >= count))
    parts = [(lambda: fine_keys[...], lambda: fine_values[...], inside, exact)]

    def write(head, mean):
        total = near[head] + gate_of(columns, head, 1) * mean
        mixed[pl.ds(head, TILE, stride=HEADS), :] = total

    attention_into(write, safe[0] > 0, query, parts)
    out[...] = mixed[...].astype(jnp.bfloat16)


def whole(a):
    return pl.BlockSpec(a.shape, lambda i: (0,) * a.ndim, pipeline_mode=pl.Buffered(1))


def by_tile(kernel, name, keys, ins, specs, out_spec, out_shape, scratch, limit=VMEM_LIMIT):
    query = pl.BlockSpec((HEADS, DK, TILE), lambda i: (0, 0, i))
    gate = pl.BlockSpec((3 * HEADS, TILE), lambda i: (0, i))
    kinds = {"scalar": smem(), "query": query, "gate": gate, "near": near_spec()}
    return pl.pallas_call(
        kernel,
        grid=(TILES,),
        in_specs=[kinds[s] if isinstance(s, str) else s for s in specs],
        out_specs=out_spec,
        out_shape=out_shape,
        scratch_shapes=scratch,
        compiler_params=pltpu.CompilerParams(
            dimension_semantics=("arbitrary",), vmem_limit_bytes=limit
        ),
        cost_estimate=pl.CostEstimate(
            flops=SEG * HEADS * keys * 1024, bytes_accessed=12 << 20, transcendentals=SEG * HEADS * keys
        ),
        name=name,
    )(*ins)


def near_spec():
    return pl.BlockSpec((HEADS, TILE, DV), lambda i: (0, i, 0))


NEAR = jax.ShapeDtypeStruct((HEADS, SEG, DV), jnp.float32)


def window_of(place, longest_query, query, previous, packed):
    return by_tile(
        window_kernel, "window", WINDOW + TILE,
        (place, longest_query, query, previous, packed),
        ["scalar", "scalar", "query", whole(previous), whole(packed)],
        near_spec(), NEAR,
        [
            pltpu.VMEM((2 * SEG, DK), jnp.bfloat16),
            pltpu.VMEM((2 * SEG, 256), jnp.bfloat16),
            pltpu.SMEM((1,), jnp.int32),
        ],
    )


def coarse_of(place, safe, query, coarse, gates, near):
    return by_tile(
        coarse_kernel, "coarse", coarse.shape[0],
        (place, safe, query, coarse, gates, near),
        ["scalar", "scalar", "query", whole(coarse), "gate", "near"],
        near_spec(), NEAR, [],
    )


def fine_of(safe, lists, query, received, packed, near, gates):
    anywhere = pl.BlockSpec(memory_space=pl.ANY)
    return by_tile(
        fine_kernel, "fine", NSEL * BLK_S,
        (safe, lists, query, received, packed, near, gates),
        ["scalar", "scalar", "query", anywhere, anywhere, "near", "gate"],
        pl.BlockSpec((TILE * HEADS, DV), lambda i: (i, 0)),
        jax.ShapeDtypeStruct((SEG * HEADS, DV), jnp.bfloat16),
        [
            pltpu.VMEM((received.shape[0] + BLOCKS, PACK, 128), jnp.bfloat16),
            pltpu.VMEM((NSEL * BLK_S, DK), jnp.bfloat16),
            pltpu.VMEM((NSEL * BLK_S, 256), jnp.bfloat16),
            pltpu.VMEM((TILE * HEADS, DV), jnp.float32),
            pltpu.SemaphoreType.DMA((2,)),
        ],
        limit=52 << 20,
    )


def on_device(
    tokens_x, gate_weight, queries, keys, values, comp_key_weight, comp_value_weight, selected
):
    segments = lax.axis_size(CTX_SEG)
    place = lax.axis_index(CTX_SEG).astype(jnp.int32).reshape(1)
    packed, coarse_own = packed_of(
        keys[:, 0].T, values[:, 0], comp_key_weight[0], comp_value_weight[0]
    )
    previous = lax.ppermute(packed, CTX_SEG, [(i, i + 1) for i in range(segments - 1)])
    coarse_part = lax.all_gather(coarse_own, ("ctx_0", "seg"), tiled=True)
    request = request_of(selected, segments)
    asked = lax.all_to_all(request, CTX_SEG, split_axis=0, concat_axis=0, tiled=True)
    reply = reply_of(asked, packed)
    logits = jnp.einsum("hcd,td->cht", gate_weight, tokens_x, preferred_element_type=jnp.float32)
    reply, coarse_part, previous, _ = lax.optimization_barrier(
        (reply, coarse_part, previous, logits)
    )
    coarse = lax.all_gather(coarse_part[:, 0:512], "ctx_1")
    coarse = coarse.reshape(lax.axis_size("ctx_1"), lax.axis_size("ctx_0"), -1, 512)
    coarse = coarse.transpose(1, 0, 2, 3).reshape(-1, 512)
    received = lax.all_to_all(reply, CTX_SEG, split_axis=0, concat_axis=0, tiled=True)
    lists = lists_of(place, selected, segments + BLOCKS)
    logits = lax.psum_scatter(logits, "head", scatter_dimension=1, tiled=True)
    gates = jax.nn.sigmoid(logits).reshape(3 * HEADS, SEG)
    query = queries.transpose(1, 2, 0)
    longest_query = jnp.max(jnp.sum(jnp.square(query.astype(jnp.float32)), axis=1))
    longest_key = jnp.max(coarse[:, DK].astype(jnp.float32))
    safe = longest_query * longest_key <= LIMIT
    safe = safe.astype(jnp.int32).reshape(1)
    near = window_of(place, longest_query.reshape(1), query, previous, packed)
    near = coarse_of(place, safe, query, coarse, gates, near)
    out = fine_of(safe, lists, query, received, packed, near, gates)
    return out.reshape(SEG, HEADS, DV)


def solution(mesh):
    split = Mesh(
        mesh.devices.reshape(4, 8, mesh.shape["head"], mesh.shape["seg"]),
        ("ctx_0", "ctx_1", "head", "seg"),
    )
    placed = (
        P(CTX_SEG, "head"),
        P(None, None, "head"),
        P(CTX_SEG, "head", None),
        P(CTX_SEG, "head", None),
        P(CTX_SEG, "head", None),
        P("head", None, None),
        P("head", None, None),
        P(CTX_SEG, "head", None),
    )
    return jax.shard_map(
        on_device, mesh=split, in_specs=placed, out_specs=P(CTX_SEG, "head", None), check_vma=False
    )
```

```python
import jax
import jax.numpy as jnp
from jax import lax
from jax.experimental import pallas as pl
from jax.experimental.pallas import tpu as pltpu
from jax.sharding import Mesh
from jax.sharding import PartitionSpec as P

TILE = 128
BLK_S = 64
BLK_C = 32
NSEL = 16
WINDOW = 512
CTX_SEG = ("ctx_0", "ctx_1", "seg")

SEG = 512
HEADS = 16
DK = 192
DV = 128
BLOCKS = SEG // BLK_S
COARSE = SEG // BLK_C
PACK = 160
TILES = SEG // TILE
TILE_BLOCKS = TILE // BLK_S
FAR = NSEL - TILE_BLOCKS
PAIRS = HEADS // 2
WIDE = 3072
NEG = -1e30
VMEM_LIMIT = 60 << 20
FLOOR = -1e29
TINY = 1e-35
SCALE2 = (DK**-0.5) * 1.4426950408889634
REACH = 96.0
LIMIT = (REACH / SCALE2) ** 2


def nn(a, b):
    return lax.dot_general(a, b, (((1,), (0,)), ((), ())), preferred_element_type=jnp.float32)


def tn(a, b):
    return lax.dot_general(a, b, (((0,), (0,)), ((), ())), preferred_element_type=jnp.float32)


def smem():
    return pl.BlockSpec(memory_space=pltpu.SMEM)


def ask_kernel(selected, request):
    for i in range(request.shape[0]):
        request[i, 0, 0] = -1
    for tile in range(TILES):
        for entry in range(NSEL):
            block = jnp.maximum(selected[tile, 0, entry], 0)
            request[lax.shift_right_logical(block, 3), 0, 0] = block & (BLOCKS - 1)


def request_of(selected, segments):
    return pl.pallas_call(
        ask_kernel,
        in_specs=[smem()],
        out_specs=smem(),
        out_shape=jax.ShapeDtypeStruct((segments, 1, 1), jnp.int32),
        name="ask",
    )(selected)


def list_kernel(pool, place, selected, lists):
    here = place[0]

    @pl.loop(0, TILES)
    def _(tile):
        own = here * BLOCKS + tile * TILE_BLOCKS
        at = jnp.int32(0)
        for entry in range(NSEL):
            lists[tile, entry] = 0
        for entry in range(NSEL):
            block = selected[tile, 0, entry]
            wanted = (block >= 0) & (block < own) & (at < FAR)
            owner = jnp.maximum(block, 0) // BLOCKS

            @pl.when(wanted)
            def _():
                lists[tile, at] = jnp.where(owner == here, pool - BLOCKS + block % BLOCKS, owner)

            at = at + wanted.astype(jnp.int32)
        lists[tile, NSEL - 1] = at


def lists_of(place, selected, pool):
    def kernel(*refs):
        list_kernel(pool, *refs)

    return pl.pallas_call(
        kernel,
        in_specs=[smem(), smem()],
        out_specs=smem(),
        out_shape=jax.ShapeDtypeStruct((TILES, NSEL), jnp.int32),
        name="lists",
    )(place, selected)


def pack_kernel(keys, values, key_weight, value_weight, packed, coarse):
    k = keys[...].T
    v = values[...]
    for b in range(BLOCKS):
        kb = k[b * BLK_S : (b + 1) * BLK_S]
        packed[b, 0:64, :] = kb[:, 0:128]
        packed[b, 64:96, :] = jnp.concatenate([kb[0:32, 128:192], kb[32:64, 128:192]], axis=1)
        packed[b, 96:160, :] = v[b * BLK_S : (b + 1) * BLK_S]
    kf = k.astype(jnp.float32)
    vf = v.astype(jnp.float32).reshape(COARSE, BLK_C, DV)
    weighted = kf.reshape(COARSE, BLK_C, DK) * key_weight[...].astype(jnp.float32)[None]
    ck = jnp.sum(weighted, axis=1)
    cv = jnp.sum(vf * value_weight[...].astype(jnp.float32)[None], axis=1)
    kt = keys[...].astype(jnp.float32)
    longest = jnp.max(jnp.sum(kt * kt, axis=0, keepdims=True), axis=1, keepdims=True)
    longest_c = jnp.max(jnp.sum(ck * ck, axis=1, keepdims=True), axis=0, keepdims=True)
    bound = jnp.maximum(longest, longest_c) * 1.02
    coarse[:, 0:DK] = ck.astype(jnp.bfloat16)
    coarse[:, DK:256] = jnp.broadcast_to(bound, (COARSE, 256 - DK)).astype(jnp.bfloat16)
    coarse[:, 256:384] = cv.astype(jnp.bfloat16)
    coarse[:, 384:512] = jnp.ones((COARSE, 128), jnp.bfloat16)
    coarse[:, 512:] = jnp.zeros((COARSE, WIDE - 512), jnp.bfloat16)


def packed_of(keys, values, key_weight, value_weight):
    return pl.pallas_call(
        pack_kernel,
        out_shape=(
            jax.ShapeDtypeStruct((BLOCKS, PACK, 128), jnp.bfloat16),
            jax.ShapeDtypeStruct((COARSE, WIDE), jnp.bfloat16),
        ),
        cost_estimate=pl.CostEstimate(flops=400000, bytes_accessed=1 << 20, transcendentals=0),
        name="pack",
    )(keys, values, key_weight, value_weight)


def reply_kernel(asked, packed, out):
    for i in range(out.shape[0]):
        out[i] = packed[jnp.maximum(asked[i, 0, 0], 0)]


def reply_of(asked, packed):
    count = asked.shape[0]
    return pl.pallas_call(
        reply_kernel,
        out_shape=jax.ShapeDtypeStruct((count, PACK, 128), jnp.bfloat16),
        in_specs=[smem(), pl.BlockSpec(memory_space=pltpu.VMEM)],
        out_specs=pl.BlockSpec(memory_space=pltpu.VMEM),
        cost_estimate=pl.CostEstimate(flops=0, bytes_accessed=3 << 20, transcendentals=0),
        name="reply",
    )(asked, packed)


def unpacked(source, keys, values, rows, present=None):
    keys[rows, 0:128] = source[0:64, :]
    tail = source[64:96, :]
    keys[rows, 128:192] = jnp.concatenate([tail[:, 0:64], tail[:, 64:128]], axis=0)
    values[rows, 0:DV] = source[96:160, :]
    values[rows, DV:] = jnp.ones((BLK_S, 128), jnp.bfloat16)


def query_pair(ref, pair):
    return jnp.concatenate([ref[2 * pair], ref[2 * pair + 1]], axis=1)


def summed_near_zero(q, parts):
    total = None
    for keys, values, mask, _ in parts:
        weights = jnp.exp2(nn(keys(), q) * SCALE2)
        if mask is not None:
            weights = jnp.where(mask(), weights, 0.0)
        term = tn(weights.astype(jnp.bfloat16), values())
        total = term if total is None else total + term
    return total


def summed_from_top(q, parts):
    scores = [jnp.where(mask(), nn(keys(), q), NEG) for keys, _, _, mask in parts]
    top = jnp.full((1, 2 * TILE), FLOOR, jnp.float32)
    for s in scores:
        top = jnp.maximum(top, jnp.max(s, axis=0, keepdims=True))
    total = None
    for s, (_, values, _, _) in zip(scores, parts):
        term = tn(jnp.exp2((s - top) * SCALE2).astype(jnp.bfloat16), values())
        total = term if total is None else total + term
    return total


def attention_into(write, safe, query, parts):
    def one(pair, summed):
        total = summed(query_pair(query, pair), parts)
        mean = total[:, 0:DV] / jnp.maximum(total[:, DV:], TINY)
        write(2 * pair, mean[0:TILE])
        write(2 * pair + 1, mean[TILE:])

    @pl.when(safe)
    def _():
        for pair in range(PAIRS):
            one(pair, summed_near_zero)

    @pl.when(jnp.logical_not(safe))
    def _():
        @pl.loop(0, PAIRS)
        def _(pair):
            one(pair, summed_from_top)


def gate_columns(gates):
    return gates[...].T


def gate_of(columns, head, branch):
    at = branch * HEADS + head
    if isinstance(at, int):
        return columns[:, at : at + 1]
    lane = lax.broadcasted_iota(jnp.int32, (TILE, 3 * HEADS), 1)
    return jnp.sum(jnp.where(lane == at, columns, 0.0), axis=1, keepdims=True)


def token_row():
    return lax.broadcasted_iota(jnp.int32, (1, 2 * TILE), 1) % TILE


def key_column(count):
    return lax.broadcasted_iota(jnp.int32, (count, 1), 0)


def window_kernel(
    place, longest_query, query, previous, packed, out, near_keys, near_values, safe
):
    tile = pl.program_id(0)
    here = place[0]

    @pl.when(tile == 0)
    def _():
        for b in range(BLOCKS):
            unpacked(packed.at[b], near_keys, near_values, pl.ds(SEG + b * BLK_S, BLK_S))

        @pl.when(here > 0)
        def _():
            for b in range(BLOCKS):
                unpacked(previous.at[b], near_keys, near_values, pl.ds(b * BLK_S, BLK_S))

        @pl.when(here == 0)
        def _():
            near_keys[0:SEG, :] = jnp.zeros((SEG, DK), jnp.bfloat16)
            near_values[0:SEG, :] = jnp.zeros((SEG, 256), jnp.bfloat16)

        wide = near_keys[...].astype(jnp.float32)
        longest = jnp.max(jnp.sum(wide * wide, axis=1, keepdims=True))
        safe[0] = (longest * longest_query[0] <= LIMIT).astype(jnp.int32)

    first = pl.multiple_of(tile * TILE, TILE)
    token = token_row()
    from_row = jnp.maximum(token, jnp.where(here > 0, 0, SEG) - first - 1)

    def part(start, count, mask, exact):
        rows = pl.ds(first + start, count)
        return (lambda: near_keys[rows, :], lambda: near_values[rows, :], mask, exact)

    after = lambda start, count: lambda: key_column(count) + start > from_row
    inside = lambda: key_column(TILE) <= token
    parts = [
        part(0, TILE, lambda: key_column(TILE) > token, after(0, TILE)),
        part(TILE, WINDOW - TILE, None, after(TILE, WINDOW - TILE)),
        part(WINDOW, TILE, inside, inside),
    ]

    def write(head, mean):
        out[head] = mean

    attention_into(write, safe[0] > 0, query, parts)


def coarse_kernel(place, safe, query, coarse, gates, near, out):
    token = token_row()
    ended = (place[0] * SEG + pl.program_id(0) * TILE + token + 1) // BLK_C
    mask = lambda: key_column(coarse.shape[0]) < ended
    columns = gate_columns(gates)
    parts = [(lambda: coarse[:, 0:DK], lambda: coarse[:, 256:512], mask, mask)]

    def write(head, mean):
        window = gate_of(columns, head, 2) * near[head]
        out[head] = gate_of(columns, head, 0) * mean + window

    attention_into(write, safe[0] > 0, query, parts)


def fine_kernel(
    safe, lists, query, received, packed, near, gates, out, pool, fine_keys, fine_values, mixed, sems
):
    tile = pl.program_id(0)
    others = received.shape[0]

    @pl.when(tile == 0)
    def _():
        copies = [
            pltpu.make_async_copy(received, pool.at[pl.ds(0, others)], sems.at[0]),
            pltpu.make_async_copy(packed, pool.at[pl.ds(others, BLOCKS)], sems.at[1]),
        ]
        for copy in copies:
            copy.start()
        for copy in copies:
            copy.wait()

    live = lists[tile, NSEL - 1]
    for entry in range(NSEL):
        if entry < FAR:
            at = lists[tile, entry]
            present = jnp.where(entry < live, 1.0, 0.0)
        else:
            at = others + tile * TILE_BLOCKS + entry - FAR
            present = 1.0
        rows = pl.ds(entry * BLK_S, BLK_S)
        fine_keys[rows, 0:128] = pool[at, 0:64, :]
        tail = pool[at, 64:96, :]
        fine_keys[rows, 128:192] = jnp.concatenate([tail[:, 0:64], tail[:, 64:128]], axis=0)
        ones = jnp.full((BLK_S, 128), present, jnp.float32).astype(jnp.bfloat16)
        fine_values[rows, 0:DV] = pool[at, 96:160, :] * ones
        fine_values[rows, DV:] = ones

    count = FAR * BLK_S
    token = token_row()
    columns = gate_columns(gates)
    row = lambda: key_column(NSEL * BLK_S)
    inside = lambda: row() <= token + count
    exact = lambda: inside() & ((row() < live * BLK_S) | (row() >= count))
    parts = [(lambda: fine_keys[...], lambda: fine_values[...], inside, exact)]

    def write(head, mean):
        total = near[head] + gate_of(columns, head, 1) * mean
        mixed[pl.ds(head, TILE, stride=HEADS), :] = total

    attention_into(write, safe[0] > 0, query, parts)
    out[...] = mixed[...].astype(jnp.bfloat16)


def whole(a):
    return pl.BlockSpec(a.shape, lambda i: (0,) * a.ndim, pipeline_mode=pl.Buffered(1))


def by_tile(kernel, name, keys, ins, specs, out_spec, out_shape, scratch, limit=VMEM_LIMIT):
    query = pl.BlockSpec((HEADS, DK, TILE), lambda i: (0, 0, i))
    gate = pl.BlockSpec((3 * HEADS, TILE), lambda i: (0, i))
    kinds = {"scalar": smem(), "query": query, "gate": gate, "near": near_spec()}
    return pl.pallas_call(
        kernel,
        grid=(TILES,),
        in_specs=[kinds[s] if isinstance(s, str) else s for s in specs],
        out_specs=out_spec,
        out_shape=out_shape,
        scratch_shapes=scratch,
        compiler_params=pltpu.CompilerParams(
            dimension_semantics=("arbitrary",), vmem_limit_bytes=limit
        ),
        cost_estimate=pl.CostEstimate(
            flops=SEG * HEADS * keys * 1024, bytes_accessed=12 << 20, transcendentals=SEG * HEADS * keys
        ),
        name=name,
    )(*ins)


def near_spec():
    return pl.BlockSpec((HEADS, TILE, DV), lambda i: (0, i, 0))


NEAR = jax.ShapeDtypeStruct((HEADS, SEG, DV), jnp.float32)


def window_of(place, longest_query, query, previous, packed):
    return by_tile(
        window_kernel, "window", WINDOW + TILE,
        (place, longest_query, query, previous, packed),
        ["scalar", "scalar", "query", whole(previous), whole(packed)],
        near_spec(), NEAR,
        [
            pltpu.VMEM((2 * SEG, DK), jnp.bfloat16),
            pltpu.VMEM((2 * SEG, 256), jnp.bfloat16),
            pltpu.SMEM((1,), jnp.int32),
        ],
    )


def coarse_of(place, safe, query, coarse, gates, near):
    return by_tile(
        coarse_kernel, "coarse", coarse.shape[0],
        (place, safe, query, coarse, gates, near),
        ["scalar", "scalar", "query", whole(coarse), "gate", "near"],
        near_spec(), NEAR, [],
    )


def fine_of(safe, lists, query, received, packed, near, gates):
    anywhere = pl.BlockSpec(memory_space=pl.ANY)
    return by_tile(
        fine_kernel, "fine", NSEL * BLK_S,
        (safe, lists, query, received, packed, near, gates),
        ["scalar", "scalar", "query", anywhere, anywhere, "near", "gate"],
        pl.BlockSpec((TILE * HEADS, DV), lambda i: (i, 0)),
        jax.ShapeDtypeStruct((SEG * HEADS, DV), jnp.bfloat16),
        [
            pltpu.VMEM((received.shape[0] + BLOCKS, PACK, 128), jnp.bfloat16),
            pltpu.VMEM((NSEL * BLK_S, DK), jnp.bfloat16),
            pltpu.VMEM((NSEL * BLK_S, 256), jnp.bfloat16),
            pltpu.VMEM((TILE * HEADS, DV), jnp.float32),
            pltpu.SemaphoreType.DMA((2,)),
        ],
        limit=52 << 20,
    )


def on_device(
    tokens_x, gate_weight, queries, keys, values, comp_key_weight, comp_value_weight, selected
):
    segments = lax.axis_size(CTX_SEG)
    place = lax.axis_index(CTX_SEG).astype(jnp.int32).reshape(1)
    packed, coarse_own = packed_of(
        keys[:, 0].T, values[:, 0], comp_key_weight[0], comp_value_weight[0]
    )
    previous = lax.ppermute(packed, CTX_SEG, [(i, i + 1) for i in range(segments - 1)])
    coarse_part = lax.all_gather(coarse_own, ("ctx_1", "seg"), tiled=True)
    request = request_of(selected, segments)
    asked = lax.all_to_all(request, CTX_SEG, split_axis=0, concat_axis=0, tiled=True)
    reply = reply_of(asked, packed)
    logits = jnp.einsum("hcd,td->cht", gate_weight, tokens_x, preferred_element_type=jnp.float32)
    reply, previous, _ = lax.optimization_barrier((reply, previous, logits))
    coarse = lax.all_gather(coarse_part[:, 0:512], "ctx_0", tiled=True)
    received = lax.all_to_all(reply, CTX_SEG, split_axis=0, concat_axis=0, tiled=True)
    previous, _ = lax.optimization_barrier((previous, coarse_part))
    lists = lists_of(place, selected, segments + BLOCKS)
    logits = lax.psum_scatter(logits, "head", scatter_dimension=1, tiled=True)
    gates = jax.nn.sigmoid(logits).reshape(3 * HEADS, SEG)
    query = queries.transpose(1, 2, 0)
    longest_query = jnp.max(jnp.sum(jnp.square(query.astype(jnp.float32)), axis=1))
    longest_key = jnp.max(coarse[:, DK].astype(jnp.float32))
    safe = longest_query * longest_key <= LIMIT
    safe = safe.astype(jnp.int32).reshape(1)
    near = window_of(place, longest_query.reshape(1), query, previous, packed)
    near = coarse_of(place, safe, query, coarse, gates, near)
    out = fine_of(safe, lists, query, received, packed, near, gates)
    return out.reshape(SEG, HEADS, DV)


def solution(mesh):
    split = Mesh(
        mesh.devices.reshape(4, 8, mesh.shape["head"], mesh.shape["seg"]),
        ("ctx_0", "ctx_1", "head", "seg"),
    )
    placed = (
        P(CTX_SEG, "head"),
        P(None, None, "head"),
        P(CTX_SEG, "head", None),
        P(CTX_SEG, "head", None),
        P(CTX_SEG, "head", None),
        P("head", None, None),
        P("head", None, None),
        P(CTX_SEG, "head", None),
    )
    return jax.shard_map(
        on_device, mesh=split, in_specs=placed, out_specs=P(CTX_SEG, "head", None), check_vma=False
    )
```

```python
import jax
import jax.numpy as jnp
from jax import lax
from jax.experimental import pallas as pl
from jax.experimental.pallas import tpu as pltpu
from jax.sharding import Mesh
from jax.sharding import PartitionSpec as P

TILE = 128
BLK_S = 64
BLK_C = 32
NSEL = 16
WINDOW = 512
CTX_SEG = ("ctx_0", "ctx_1", "seg")

SEG = 512
HEADS = 16
DK = 192
DV = 128
BLOCKS = SEG // BLK_S
COARSE = SEG // BLK_C
PACK = 160
TILES = SEG // TILE
TILE_BLOCKS = TILE // BLK_S
FAR = NSEL - TILE_BLOCKS
PAIRS = HEADS // 2
WIDE = 3072
NEG = -1e30
VMEM_LIMIT = 60 << 20
FLOOR = -1e29
TINY = 1e-35
SCALE2 = (DK**-0.5) * 1.4426950408889634
REACH = 96.0
LIMIT = (REACH / SCALE2) ** 2


def nn(a, b):
    return lax.dot_general(a, b, (((1,), (0,)), ((), ())), preferred_element_type=jnp.float32)


def tn(a, b):
    return lax.dot_general(a, b, (((0,), (0,)), ((), ())), preferred_element_type=jnp.float32)


def smem():
    return pl.BlockSpec(memory_space=pltpu.SMEM)


def list_kernel(pool, place, selected, lists):
    here = place[0]

    @pl.loop(0, TILES)
    def _(tile):
        own = here * BLOCKS + tile * TILE_BLOCKS
        at = jnp.int32(0)
        for entry in range(NSEL):
            lists[tile, entry] = 0
        for entry in range(NSEL):
            block = selected[tile, 0, entry]
            wanted = (block >= 0) & (block < own) & (at < FAR)
            owner = jnp.maximum(block, 0) // BLOCKS

            @pl.when(wanted)
            def _():
                lists[tile, at] = jnp.where(owner == here, pool - BLOCKS + block % BLOCKS, owner)

            at = at + wanted.astype(jnp.int32)
        lists[tile, NSEL - 1] = at


def lists_of(place, selected, pool):
    def kernel(*refs):
        list_kernel(pool, *refs)

    return pl.pallas_call(
        kernel,
        in_specs=[smem(), smem()],
        out_specs=smem(),
        out_shape=jax.ShapeDtypeStruct((TILES, NSEL), jnp.int32),
        name="lists",
    )(place, selected)


def pack_kernel(selected, keys, values, key_weight, value_weight, packed, coarse, request):
    for i in range(request.shape[0]):
        request[i, 0, 0] = -1
    for tile in range(TILES):
        for entry in range(NSEL):
            block = jnp.maximum(selected[tile, 0, entry], 0)
            request[lax.shift_right_logical(block, 3), 0, 0] = block & (BLOCKS - 1)
    k = keys[...].T
    v = values[...]
    for b in range(BLOCKS):
        kb = k[b * BLK_S : (b + 1) * BLK_S]
        packed[b, 0:64, :] = kb[:, 0:128]
        packed[b, 64:96, :] = jnp.concatenate([kb[0:32, 128:192], kb[32:64, 128:192]], axis=1)
        packed[b, 96:160, :] = v[b * BLK_S : (b + 1) * BLK_S]
    kf = k.astype(jnp.float32)
    vf = v.astype(jnp.float32).reshape(COARSE, BLK_C, DV)
    weighted = kf.reshape(COARSE, BLK_C, DK) * key_weight[...].astype(jnp.float32)[None]
    ck = jnp.sum(weighted, axis=1)
    cv = jnp.sum(vf * value_weight[...].astype(jnp.float32)[None], axis=1)
    kt = keys[...].astype(jnp.float32)
    longest = jnp.max(jnp.sum(kt * kt, axis=0, keepdims=True), axis=1, keepdims=True)
    longest_c = jnp.max(jnp.sum(ck * ck, axis=1, keepdims=True), axis=0, keepdims=True)
    bound = jnp.maximum(longest, longest_c) * 1.02
    coarse[:, 0:DK] = ck.astype(jnp.bfloat16)
    coarse[:, DK:256] = jnp.broadcast_to(bound, (COARSE, 256 - DK)).astype(jnp.bfloat16)
    coarse[:, 256:384] = cv.astype(jnp.bfloat16)
    coarse[:, 384:512] = jnp.ones((COARSE, 128), jnp.bfloat16)
    coarse[:, 512:] = jnp.zeros((COARSE, WIDE - 512), jnp.bfloat16)


def packed_of(selected, keys, values, key_weight, value_weight, segments):
    return pl.pallas_call(
        pack_kernel,
        out_shape=(
            jax.ShapeDtypeStruct((BLOCKS, PACK, 128), jnp.bfloat16),
            jax.ShapeDtypeStruct((COARSE, WIDE), jnp.bfloat16),
            jax.ShapeDtypeStruct((segments, 1, 1), jnp.int32),
        ),
        in_specs=[smem()] + [pl.BlockSpec(memory_space=pltpu.VMEM)] * 4,
        out_specs=(
            pl.BlockSpec(memory_space=pltpu.VMEM), pl.BlockSpec(memory_space=pltpu.VMEM), smem()
        ),
        cost_estimate=pl.CostEstimate(flops=400000, bytes_accessed=1 << 20, transcendentals=0),
        name="pack",
    )(selected, keys, values, key_weight, value_weight)


def reply_kernel(asked, packed, out):
    for i in range(out.shape[0]):
        out[i] = packed[jnp.maximum(asked[i, 0, 0], 0)]


def reply_of(asked, packed):
    count = asked.shape[0]
    return pl.pallas_call(
        reply_kernel,
        out_shape=jax.ShapeDtypeStruct((count, PACK, 128), jnp.bfloat16),
        in_specs=[smem(), pl.BlockSpec(memory_space=pltpu.VMEM)],
        out_specs=pl.BlockSpec(memory_space=pltpu.VMEM),
        cost_estimate=pl.CostEstimate(flops=0, bytes_accessed=3 << 20, transcendentals=0),
        name="reply",
    )(asked, packed)


def unpacked(source, keys, values, rows, present=None):
    keys[rows, 0:128] = source[0:64, :]
    tail = source[64:96, :]
    keys[rows, 128:192] = jnp.concatenate([tail[:, 0:64], tail[:, 64:128]], axis=0)
    values[rows, 0:DV] = source[96:160, :]
    values[rows, DV:] = jnp.ones((BLK_S, 128), jnp.bfloat16)


def query_pair(ref, pair):
    return jnp.concatenate([ref[2 * pair], ref[2 * pair + 1]], axis=1)


def summed_near_zero(q, parts):
    total = None
    for keys, values, mask, _ in parts:
        weights = jnp.exp2(nn(keys(), q) * SCALE2)
        if mask is not None:
            weights = jnp.where(mask(), weights, 0.0)
        term = tn(weights.astype(jnp.bfloat16), values())
        total = term if total is None else total + term
    return total


def summed_from_top(q, parts):
    scores = [jnp.where(mask(), nn(keys(), q), NEG) for keys, _, _, mask in parts]
    top = jnp.full((1, 2 * TILE), FLOOR, jnp.float32)
    for s in scores:
        top = jnp.maximum(top, jnp.max(s, axis=0, keepdims=True))
    total = None
    for s, (_, values, _, _) in zip(scores, parts):
        term = tn(jnp.exp2((s - top) * SCALE2).astype(jnp.bfloat16), values())
        total = term if total is None else total + term
    return total


def attention_into(write, safe, query, parts):
    def one(pair, summed):
        total = summed(query_pair(query, pair), parts)
        mean = total[:, 0:DV] / jnp.maximum(total[:, DV:], TINY)
        write(2 * pair, mean[0:TILE])
        write(2 * pair + 1, mean[TILE:])

    @pl.when(safe)
    def _():
        for pair in range(PAIRS):
            one(pair, summed_near_zero)

    @pl.when(jnp.logical_not(safe))
    def _():
        @pl.loop(0, PAIRS)
        def _(pair):
            one(pair, summed_from_top)


def gate_columns(gates):
    return gates[...].T


def gate_of(columns, head, branch):
    at = branch * HEADS + head
    if isinstance(at, int):
        return columns[:, at : at + 1]
    lane = lax.broadcasted_iota(jnp.int32, (TILE, 3 * HEADS), 1)
    return jnp.sum(jnp.where(lane == at, columns, 0.0), axis=1, keepdims=True)


def token_row():
    return lax.broadcasted_iota(jnp.int32, (1, 2 * TILE), 1) % TILE


def key_column(count):
    return lax.broadcasted_iota(jnp.int32, (count, 1), 0)


def window_kernel(
    place, longest_query, query, previous, packed, out, near_keys, near_values, safe
):
    tile = pl.program_id(0)
    here = place[0]

    @pl.when(tile == 0)
    def _():
        for b in range(BLOCKS):
            unpacked(packed.at[b], near_keys, near_values, pl.ds(SEG + b * BLK_S, BLK_S))

        @pl.when(here > 0)
        def _():
            for b in range(BLOCKS):
                unpacked(previous.at[b], near_keys, near_values, pl.ds(b * BLK_S, BLK_S))

        @pl.when(here == 0)
        def _():
            near_keys[0:SEG, :] = jnp.zeros((SEG, DK), jnp.bfloat16)
            near_values[0:SEG, :] = jnp.zeros((SEG, 256), jnp.bfloat16)

        wide = near_keys[...].astype(jnp.float32)
        longest = jnp.max(jnp.sum(wide * wide, axis=1, keepdims=True))
        safe[0] = (longest * longest_query[0] <= LIMIT).astype(jnp.int32)

    first = pl.multiple_of(tile * TILE, TILE)
    token = token_row()
    from_row = jnp.maximum(token, jnp.where(here > 0, 0, SEG) - first - 1)

    def part(start, count, mask, exact):
        rows = pl.ds(first + start, count)
        return (lambda: near_keys[rows, :], lambda: near_values[rows, :], mask, exact)

    after = lambda start, count: lambda: key_column(count) + start > from_row
    inside = lambda: key_column(TILE) <= token
    parts = [
        part(0, TILE, lambda: key_column(TILE) > token, after(0, TILE)),
        part(TILE, WINDOW - TILE, None, after(TILE, WINDOW - TILE)),
        part(WINDOW, TILE, inside, inside),
    ]

    def write(head, mean):
        out[head] = mean

    attention_into(write, safe[0] > 0, query, parts)


def coarse_kernel(place, safe, query, coarse, gates, near, out):
    token = token_row()
    ended = (place[0] * SEG + pl.program_id(0) * TILE + token + 1) // BLK_C
    mask = lambda: key_column(coarse.shape[0]) < ended
    columns = gate_columns(gates)
    parts = [(lambda: coarse[:, 0:DK], lambda: coarse[:, 256:512], mask, mask)]

    def write(head, mean):
        window = gate_of(columns, head, 2) * near[head]
        out[head] = gate_of(columns, head, 0) * mean + window

    attention_into(write, safe[0] > 0, query, parts)


def fine_kernel(
    safe, lists, query, received, packed, near, gates, out, pool, fine_keys, fine_values, mixed, sems
):
    tile = pl.program_id(0)
    others = received.shape[0]

    @pl.when(tile == 0)
    def _():
        copies = [
            pltpu.make_async_copy(received, pool.at[pl.ds(0, others)], sems.at[0]),
            pltpu.make_async_copy(packed, pool.at[pl.ds(others, BLOCKS)], sems.at[1]),
        ]
        for copy in copies:
            copy.start()
        for copy in copies:
            copy.wait()

    live = lists[tile, NSEL - 1]
    for entry in range(NSEL):
        if entry < FAR:
            at = lists[tile, entry]
            present = jnp.where(entry < live, 1.0, 0.0)
        else:
            at = others + tile * TILE_BLOCKS + entry - FAR
            present = 1.0
        rows = pl.ds(entry * BLK_S, BLK_S)
        fine_keys[rows, 0:128] = pool[at, 0:64, :]
        tail = pool[at, 64:96, :]
        fine_keys[rows, 128:192] = jnp.concatenate([tail[:, 0:64], tail[:, 64:128]], axis=0)
        ones = jnp.full((BLK_S, 128), present, jnp.float32).astype(jnp.bfloat16)
        fine_values[rows, 0:DV] = pool[at, 96:160, :] * ones
        fine_values[rows, DV:] = ones

    count = FAR * BLK_S
    token = token_row()
    columns = gate_columns(gates)
    row = lambda: key_column(NSEL * BLK_S)
    inside = lambda: row() <= token + count
    exact = lambda: inside() & ((row() < live * BLK_S) | (row() >= count))
    parts = [(lambda: fine_keys[...], lambda: fine_values[...], inside, exact)]

    def write(head, mean):
        total = near[head] + gate_of(columns, head, 1) * mean
        mixed[pl.ds(head, TILE, stride=HEADS), :] = total

    attention_into(write, safe[0] > 0, query, parts)
    out[...] = mixed[...].astype(jnp.bfloat16)


def whole(a):
    return pl.BlockSpec(a.shape, lambda i: (0,) * a.ndim, pipeline_mode=pl.Buffered(1))


def by_tile(kernel, name, keys, ins, specs, out_spec, out_shape, scratch, limit=VMEM_LIMIT):
    query = pl.BlockSpec((HEADS, DK, TILE), lambda i: (0, 0, i))
    gate = pl.BlockSpec((3 * HEADS, TILE), lambda i: (0, i))
    kinds = {"scalar": smem(), "query": query, "gate": gate, "near": near_spec()}
    return pl.pallas_call(
        kernel,
        grid=(TILES,),
        in_specs=[kinds[s] if isinstance(s, str) else s for s in specs],
        out_specs=out_spec,
        out_shape=out_shape,
        scratch_shapes=scratch,
        compiler_params=pltpu.CompilerParams(
            dimension_semantics=("arbitrary",), vmem_limit_bytes=limit
        ),
        cost_estimate=pl.CostEstimate(
            flops=SEG * HEADS * keys * 1024, bytes_accessed=12 << 20, transcendentals=SEG * HEADS * keys
        ),
        name=name,
    )(*ins)


def near_spec():
    return pl.BlockSpec((HEADS, TILE, DV), lambda i: (0, i, 0))


NEAR = jax.ShapeDtypeStruct((HEADS, SEG, DV), jnp.float32)


def window_of(place, longest_query, query, previous, packed):
    return by_tile(
        window_kernel, "window", WINDOW + TILE,
        (place, longest_query, query, previous, packed),
        ["scalar", "scalar", "query", whole(previous), whole(packed)],
        near_spec(), NEAR,
        [
            pltpu.VMEM((2 * SEG, DK), jnp.bfloat16),
            pltpu.VMEM((2 * SEG, 256), jnp.bfloat16),
            pltpu.SMEM((1,), jnp.int32),
        ],
    )


def coarse_of(place, safe, query, coarse, gates, near):
    return by_tile(
        coarse_kernel, "coarse", coarse.shape[0],
        (place, safe, query, coarse, gates, near),
        ["scalar", "scalar", "query", whole(coarse), "gate", "near"],
        near_spec(), NEAR, [],
    )


def fine_of(safe, lists, query, received, packed, near, gates):
    anywhere = pl.BlockSpec(memory_space=pl.ANY)
    return by_tile(
        fine_kernel, "fine", NSEL * BLK_S,
        (safe, lists, query, received, packed, near, gates),
        ["scalar", "scalar", "query", anywhere, anywhere, "near", "gate"],
        pl.BlockSpec((TILE * HEADS, DV), lambda i: (i, 0)),
        jax.ShapeDtypeStruct((SEG * HEADS, DV), jnp.bfloat16),
        [
            pltpu.VMEM((received.shape[0] + BLOCKS, PACK, 128), jnp.bfloat16),
            pltpu.VMEM((NSEL * BLK_S, DK), jnp.bfloat16),
            pltpu.VMEM((NSEL * BLK_S, 256), jnp.bfloat16),
            pltpu.VMEM((TILE * HEADS, DV), jnp.float32),
            pltpu.SemaphoreType.DMA((2,)),
        ],
        limit=52 << 20,
    )


def on_device(
    tokens_x, gate_weight, queries, keys, values, comp_key_weight, comp_value_weight, selected
):
    segments = lax.axis_size(CTX_SEG)
    place = lax.axis_index(CTX_SEG).astype(jnp.int32).reshape(1)
    packed, coarse_own, request = packed_of(
        selected, keys[:, 0].T, values[:, 0], comp_key_weight[0], comp_value_weight[0], segments
    )
    previous = lax.ppermute(packed, CTX_SEG, [(i, i + 1) for i in range(segments - 1)])
    coarse_part = lax.all_gather(coarse_own, ("ctx_1", "seg"), tiled=True)
    asked = lax.all_to_all(request, CTX_SEG, split_axis=0, concat_axis=0, tiled=True)
    reply = reply_of(asked, packed)
    logits = jnp.einsum("hcd,td->cht", gate_weight, tokens_x, preferred_element_type=jnp.float32)
    reply, previous, _ = lax.optimization_barrier((reply, previous, logits))
    coarse = lax.all_gather(coarse_part[:, 0:512], "ctx_0", tiled=True)
    received = lax.all_to_all(reply, CTX_SEG, split_axis=0, concat_axis=0, tiled=True)
    previous, _ = lax.optimization_barrier((previous, coarse_part))
    lists = lists_of(place, selected, segments + BLOCKS)
    logits = lax.psum_scatter(logits, "head", scatter_dimension=1, tiled=True)
    gates = jax.nn.sigmoid(logits).reshape(3 * HEADS, SEG)
    query = queries.transpose(1, 2, 0)
    longest_query = jnp.max(jnp.sum(jnp.square(query.astype(jnp.float32)), axis=1))
    longest_key = jnp.max(coarse[:, DK].astype(jnp.float32))
    safe = longest_query * longest_key <= LIMIT
    safe = safe.astype(jnp.int32).reshape(1)
    near = window_of(place, longest_query.reshape(1), query, previous, packed)
    near = coarse_of(place, safe, query, coarse, gates, near)
    out = fine_of(safe, lists, query, received, packed, near, gates)
    return out.reshape(SEG, HEADS, DV)


def solution(mesh):
    split = Mesh(
        mesh.devices.reshape(4, 8, mesh.shape["head"], mesh.shape["seg"]),
        ("ctx_0", "ctx_1", "head", "seg"),
    )
    placed = (
        P(CTX_SEG, "head"),
        P(None, None, "head"),
        P(CTX_SEG, "head", None),
        P(CTX_SEG, "head", None),
        P(CTX_SEG, "head", None),
        P("head", None, None),
        P("head", None, None),
        P(CTX_SEG, "head", None),
    )
    return jax.shard_map(
        on_device, mesh=split, in_specs=placed, out_specs=P(CTX_SEG, "head", None), check_vma=False
    )
```

```python
import jax
import jax.numpy as jnp
from jax import lax
from jax.experimental import pallas as pl
from jax.experimental.pallas import tpu as pltpu
from jax.sharding import Mesh
from jax.sharding import PartitionSpec as P

TILE = 128
BLK_S = 64
BLK_C = 32
NSEL = 16
WINDOW = 512
CTX_SEG = ("ctx_0", "ctx_1", "seg")

SEG = 512
HEADS = 16
DK = 192
DV = 128
BLOCKS = SEG // BLK_S
COARSE = SEG // BLK_C
PACK = 160
TILES = SEG // TILE
TILE_BLOCKS = TILE // BLK_S
FAR = NSEL - TILE_BLOCKS
PAIRS = HEADS // 2
WIDE = 3072
NEG = -1e30
VMEM_LIMIT = 60 << 20
FLOOR = -1e29
TINY = 1e-35
SPLIT = 8
SCALE2 = (DK**-0.5) * 1.4426950408889634
REACH = 96.0
LIMIT = (REACH / SCALE2) ** 2


def nn(a, b):
    return lax.dot_general(a, b, (((1,), (0,)), ((), ())), preferred_element_type=jnp.float32)


def tn(a, b):
    return lax.dot_general(a, b, (((0,), (0,)), ((), ())), preferred_element_type=jnp.float32)


def smem():
    return pl.BlockSpec(memory_space=pltpu.SMEM)


def list_kernel(pool, place, selected, lists):
    here = place[0]

    @pl.loop(0, TILES)
    def _(tile):
        own = here * BLOCKS + tile * TILE_BLOCKS
        at = jnp.int32(0)
        for entry in range(NSEL):
            lists[tile, entry] = 0
        for entry in range(NSEL):
            block = selected[tile, 0, entry]
            wanted = (block >= 0) & (block < own) & (at < FAR)
            owner = jnp.maximum(block, 0) // BLOCKS

            @pl.when(wanted)
            def _():
                lists[tile, at] = jnp.where(owner == here, pool - BLOCKS + block % BLOCKS, owner)

            at = at + wanted.astype(jnp.int32)
        lists[tile, NSEL - 1] = at


def lists_of(place, selected, pool):
    def kernel(*refs):
        list_kernel(pool, *refs)

    return pl.pallas_call(
        kernel,
        in_specs=[smem(), smem()],
        out_specs=smem(),
        out_shape=jax.ShapeDtypeStruct((TILES, NSEL), jnp.int32),
        name="lists",
    )(place, selected)


def pack_kernel(selected, keys, values, key_weight, value_weight, packed, coarse, request):
    for i in range(request.shape[0]):
        request[i, 0, 0] = -1
    for tile in range(TILES):
        for entry in range(NSEL):
            block = jnp.maximum(selected[tile, 0, entry], 0)
            request[lax.shift_right_logical(block, 3), 0, 0] = block & (BLOCKS - 1)
    k = keys[...].T
    v = values[...]
    for b in range(BLOCKS):
        kb = k[b * BLK_S : (b + 1) * BLK_S]
        packed[b, 0:64, :] = kb[:, 0:128]
        packed[b, 64:96, :] = jnp.concatenate([kb[0:32, 128:192], kb[32:64, 128:192]], axis=1)
        packed[b, 96:160, :] = v[b * BLK_S : (b + 1) * BLK_S]
    kf = k.astype(jnp.float32)
    vf = v.astype(jnp.float32).reshape(COARSE, BLK_C, DV)
    weighted = kf.reshape(COARSE, BLK_C, DK) * key_weight[...].astype(jnp.float32)[None]
    ck = jnp.sum(weighted, axis=1)
    cv = jnp.sum(vf * value_weight[...].astype(jnp.float32)[None], axis=1)
    kt = keys[...].astype(jnp.float32)
    longest = jnp.max(jnp.sum(kt * kt, axis=0, keepdims=True), axis=1, keepdims=True)
    longest_c = jnp.max(jnp.sum(ck * ck, axis=1, keepdims=True), axis=0, keepdims=True)
    bound = jnp.maximum(longest, longest_c) * 1.02
    coarse[:, 0:DK] = ck.astype(jnp.bfloat16)
    coarse[:, DK:256] = jnp.broadcast_to(bound, (COARSE, 256 - DK)).astype(jnp.bfloat16)
    coarse[:, 256:384] = cv.astype(jnp.bfloat16)
    coarse[:, 384:512] = jnp.ones((COARSE, 128), jnp.bfloat16)
    coarse[:, 512:] = jnp.zeros((COARSE, WIDE - 512), jnp.bfloat16)


def packed_of(selected, keys, values, key_weight, value_weight, segments):
    return pl.pallas_call(
        pack_kernel,
        out_shape=(
            jax.ShapeDtypeStruct((BLOCKS, PACK, 128), jnp.bfloat16),
            jax.ShapeDtypeStruct((COARSE, WIDE), jnp.bfloat16),
            jax.ShapeDtypeStruct((segments, 1, 1), jnp.int32),
        ),
        in_specs=[smem()] + [pl.BlockSpec(memory_space=pltpu.VMEM)] * 4,
        out_specs=(
            pl.BlockSpec(memory_space=pltpu.VMEM), pl.BlockSpec(memory_space=pltpu.VMEM), smem()
        ),
        cost_estimate=pl.CostEstimate(flops=400000, bytes_accessed=1 << 20, transcendentals=0),
        name="pack",
    )(selected, keys, values, key_weight, value_weight)


def reply_kernel(asked, packed, out):
    for i in range(out.shape[0]):
        out[i] = packed[jnp.maximum(asked[i, 0, 0], 0)]


def reply_of(asked, packed):
    count = asked.shape[0]
    return pl.pallas_call(
        reply_kernel,
        out_shape=jax.ShapeDtypeStruct((count, PACK, 128), jnp.bfloat16),
        in_specs=[smem(), pl.BlockSpec(memory_space=pltpu.VMEM)],
        out_specs=pl.BlockSpec(memory_space=pltpu.VMEM),
        cost_estimate=pl.CostEstimate(flops=0, bytes_accessed=3 << 20, transcendentals=0),
        name="reply",
    )(asked, packed)


def unpacked(source, keys, values, rows, present=None):
    keys[rows, 0:128] = source[0:64, :]
    tail = source[64:96, :]
    keys[rows, 128:192] = jnp.concatenate([tail[:, 0:64], tail[:, 64:128]], axis=0)
    values[rows, 0:DV] = source[96:160, :]
    values[rows, DV:] = jnp.ones((BLK_S, 128), jnp.bfloat16)


def query_pair(ref, pair):
    return jnp.concatenate([ref[2 * pair], ref[2 * pair + 1]], axis=1)


def summed_near_zero(q, parts):
    total = None
    for keys, values, mask, _ in parts:
        weights = jnp.exp2(nn(keys(), q) * SCALE2)
        if mask is not None:
            weights = jnp.where(mask(), weights, 0.0)
        term = tn(weights.astype(jnp.bfloat16), values())
        total = term if total is None else total + term
    return total


def summed_from_top(q, parts):
    scores = [jnp.where(mask(), nn(keys(), q), NEG) for keys, _, _, mask in parts]
    top = jnp.full((1, 2 * TILE), FLOOR, jnp.float32)
    for s in scores:
        top = jnp.maximum(top, jnp.max(s, axis=0, keepdims=True))
    total = None
    for s, (_, values, _, _) in zip(scores, parts):
        term = tn(jnp.exp2((s - top) * SCALE2).astype(jnp.bfloat16), values())
        total = term if total is None else total + term
    return total


def attention_into(write, safe, query, parts):
    def one(pair, summed):
        total = summed(query_pair(query, pair), parts)
        mean = total[:, 0:DV] / jnp.maximum(total[:, DV:], TINY)
        write(2 * pair, mean[0:TILE])
        write(2 * pair + 1, mean[TILE:])

    @pl.when(safe)
    def _():
        for pair in range(PAIRS):
            one(pair, summed_near_zero)

    @pl.when(jnp.logical_not(safe))
    def _():
        @pl.loop(0, PAIRS)
        def _(pair):
            one(pair, summed_from_top)


def gate_columns(gates):
    return gates[...].T


def gate_of(columns, head, branch):
    at = branch * HEADS + head
    if isinstance(at, int):
        return columns[:, at : at + 1]
    lane = lax.broadcasted_iota(jnp.int32, (TILE, 3 * HEADS), 1)
    return jnp.sum(jnp.where(lane == at, columns, 0.0), axis=1, keepdims=True)


def token_row():
    return lax.broadcasted_iota(jnp.int32, (1, 2 * TILE), 1) % TILE


def key_column(count):
    return lax.broadcasted_iota(jnp.int32, (count, 1), 0)


def window_kernel(
    place, longest_query, query, previous, packed, out, near_keys, near_values, safe
):
    tile = pl.program_id(0)
    here = place[0]

    @pl.when(tile == 0)
    def _():
        for b in range(BLOCKS):
            unpacked(packed.at[b], near_keys, near_values, pl.ds(SEG + b * BLK_S, BLK_S))

        @pl.when(here > 0)
        def _():
            for b in range(BLOCKS):
                unpacked(previous.at[b], near_keys, near_values, pl.ds(b * BLK_S, BLK_S))

        @pl.when(here == 0)
        def _():
            near_keys[0:SEG, :] = jnp.zeros((SEG, DK), jnp.bfloat16)
            near_values[0:SEG, :] = jnp.zeros((SEG, 256), jnp.bfloat16)

        wide = near_keys[...].astype(jnp.float32)
        longest = jnp.max(jnp.sum(wide * wide, axis=1, keepdims=True))
        safe[0] = (longest * longest_query[0] <= LIMIT).astype(jnp.int32)

    first = pl.multiple_of(tile * TILE, TILE)
    token = token_row()
    from_row = jnp.maximum(token, jnp.where(here > 0, 0, SEG) - first - 1)

    def part(start, count, mask, exact):
        rows = pl.ds(first + start, count)
        return (lambda: near_keys[rows, :], lambda: near_values[rows, :], mask, exact)

    after = lambda start, count: lambda: key_column(count) + start > from_row
    inside = lambda: key_column(TILE) <= token
    parts = [
        part(0, TILE, lambda: key_column(TILE) > token, after(0, TILE)),
        part(TILE, WINDOW - TILE, None, after(TILE, WINDOW - TILE)),
        part(WINDOW, TILE, inside, inside),
    ]

    def write(head, mean):
        out[head] = mean

    attention_into(write, safe[0] > 0, query, parts)


def coarse_kernel(place, longest_query, query, coarse, gates, near, out, safe_out, safe):
    @pl.when(pl.program_id(0) == 0)
    def _():
        beside = coarse[:, 128:256].astype(jnp.float32)
        lane = lax.broadcasted_iota(jnp.int32, beside.shape, 1)
        longest_key = jnp.max(jnp.where(lane >= DK - 128, beside, 0.0))
        safe[0] = (longest_key * longest_query[0] <= LIMIT).astype(jnp.int32)
        safe_out[0] = safe[0]

    token = token_row()
    ended = (place[0] * SEG + pl.program_id(0) * TILE + token + 1) // BLK_C
    mask = lambda: key_column(coarse.shape[0]) < ended
    columns = gate_columns(gates)
    parts = [(lambda: coarse[:, 0:DK], lambda: coarse[:, 256:512], mask, mask)]

    def write(head, mean):
        window = gate_of(columns, head, 2) * near[head]
        out[head] = gate_of(columns, head, 0) * mean + window

    attention_into(write, safe[0] > 0, query, parts)


def fine_kernel(
    safe, lists, query, received, packed, near, gates, out, pool, fine_keys, fine_values, mixed, sems
):
    tile = pl.program_id(0)
    others = received.shape[0]

    @pl.when(tile == 0)
    def _():
        part = others // SPLIT
        copies = [
            pltpu.make_async_copy(
                received.at[pl.ds(i * part, part)], pool.at[pl.ds(i * part, part)], sems.at[i]
            )
            for i in range(SPLIT)
        ]
        copies.append(
            pltpu.make_async_copy(packed, pool.at[pl.ds(others, BLOCKS)], sems.at[SPLIT])
        )
        for copy in copies:
            copy.start()
        for copy in copies:
            copy.wait()

    live = lists[tile, NSEL - 1]
    for entry in range(NSEL):
        if entry < FAR:
            at = lists[tile, entry]
            present = jnp.where(entry < live, 1.0, 0.0)
        else:
            at = others + tile * TILE_BLOCKS + entry - FAR
            present = 1.0
        rows = pl.ds(entry * BLK_S, BLK_S)
        fine_keys[rows, 0:128] = pool[at, 0:64, :]
        tail = pool[at, 64:96, :]
        fine_keys[rows, 128:192] = jnp.concatenate([tail[:, 0:64], tail[:, 64:128]], axis=0)
        ones = jnp.full((BLK_S, 128), present, jnp.float32).astype(jnp.bfloat16)
        fine_values[rows, 0:DV] = pool[at, 96:160, :] * ones
        fine_values[rows, DV:] = ones

    count = FAR * BLK_S
    token = token_row()
    columns = gate_columns(gates)
    row = lambda: key_column(NSEL * BLK_S)
    inside = lambda: row() <= token + count
    exact = lambda: inside() & ((row() < live * BLK_S) | (row() >= count))
    parts = [(lambda: fine_keys[...], lambda: fine_values[...], inside, exact)]

    def write(head, mean):
        total = near[head] + gate_of(columns, head, 1) * mean
        mixed[pl.ds(head, TILE, stride=HEADS), :] = total

    attention_into(write, safe[0] > 0, query, parts)
    out[...] = mixed[...].astype(jnp.bfloat16)


def whole(a):
    return pl.BlockSpec(a.shape, lambda i: (0,) * a.ndim, pipeline_mode=pl.Buffered(1))


def by_tile(kernel, name, keys, ins, specs, out_spec, out_shape, scratch, limit=VMEM_LIMIT):
    query = pl.BlockSpec((HEADS, DK, TILE), lambda i: (0, 0, i))
    gate = pl.BlockSpec((3 * HEADS, TILE), lambda i: (0, i))
    kinds = {"scalar": smem(), "query": query, "gate": gate, "near": near_spec()}
    return pl.pallas_call(
        kernel,
        grid=(TILES,),
        in_specs=[kinds[s] if isinstance(s, str) else s for s in specs],
        out_specs=out_spec,
        out_shape=out_shape,
        scratch_shapes=scratch,
        compiler_params=pltpu.CompilerParams(
            dimension_semantics=("arbitrary",), vmem_limit_bytes=limit
        ),
        cost_estimate=pl.CostEstimate(
            flops=SEG * HEADS * keys * 1024, bytes_accessed=12 << 20, transcendentals=SEG * HEADS * keys
        ),
        name=name,
    )(*ins)


def near_spec():
    return pl.BlockSpec((HEADS, TILE, DV), lambda i: (0, i, 0))


NEAR = jax.ShapeDtypeStruct((HEADS, SEG, DV), jnp.float32)


def window_of(place, longest_query, query, previous, packed):
    return by_tile(
        window_kernel, "window", WINDOW + TILE,
        (place, longest_query, query, previous, packed),
        ["scalar", "scalar", "query", whole(previous), whole(packed)],
        near_spec(), NEAR,
        [
            pltpu.VMEM((2 * SEG, DK), jnp.bfloat16),
            pltpu.VMEM((2 * SEG, 256), jnp.bfloat16),
            pltpu.SMEM((1,), jnp.int32),
        ],
    )


def coarse_of(place, longest_query, query, coarse, gates, near):
    return by_tile(
        coarse_kernel, "coarse", coarse.shape[0],
        (place, longest_query, query, coarse, gates, near),
        ["scalar", "scalar", "query", whole(coarse), "gate", "near"],
        (near_spec(), smem()), (NEAR, jax.ShapeDtypeStruct((1,), jnp.int32)),
        [pltpu.SMEM((1,), jnp.int32)],
    )


def fine_of(safe, lists, query, received, packed, near, gates):
    anywhere = pl.BlockSpec(memory_space=pl.ANY)
    return by_tile(
        fine_kernel, "fine", NSEL * BLK_S,
        (safe, lists, query, received, packed, near, gates),
        ["scalar", "scalar", "query", anywhere, anywhere, "near", "gate"],
        pl.BlockSpec((TILE * HEADS, DV), lambda i: (i, 0)),
        jax.ShapeDtypeStruct((SEG * HEADS, DV), jnp.bfloat16),
        [
            pltpu.VMEM((received.shape[0] + BLOCKS, PACK, 128), jnp.bfloat16),
            pltpu.VMEM((NSEL * BLK_S, DK), jnp.bfloat16),
            pltpu.VMEM((NSEL * BLK_S, 256), jnp.bfloat16),
            pltpu.VMEM((TILE * HEADS, DV), jnp.float32),
            pltpu.SemaphoreType.DMA((SPLIT + 1,)),
        ],
        limit=52 << 20,
    )


def on_device(
    tokens_x, gate_weight, queries, keys, values, comp_key_weight, comp_value_weight, selected
):
    segments = lax.axis_size(CTX_SEG)
    place = lax.axis_index(CTX_SEG).astype(jnp.int32).reshape(1)
    packed, coarse_own, request = packed_of(
        selected, keys[:, 0].T, values[:, 0], comp_key_weight[0], comp_value_weight[0], segments
    )
    previous = lax.ppermute(packed, CTX_SEG, [(i, i + 1) for i in range(segments - 1)])
    coarse_part = lax.all_gather(coarse_own, ("ctx_1", "seg"), tiled=True)
    asked = lax.all_to_all(request, CTX_SEG, split_axis=0, concat_axis=0, tiled=True)
    reply = reply_of(asked, packed)
    logits = jnp.einsum("hcd,td->cht", gate_weight, tokens_x, preferred_element_type=jnp.float32)
    reply, previous, _ = lax.optimization_barrier((reply, previous, logits))
    coarse = lax.all_gather(coarse_part[:, 0:512], "ctx_0", tiled=True)
    received = lax.all_to_all(reply, CTX_SEG, split_axis=0, concat_axis=0, tiled=True)
    previous, _ = lax.optimization_barrier((previous, coarse_part))
    lists = lists_of(place, selected, segments + BLOCKS)
    logits = lax.psum_scatter(logits, "head", scatter_dimension=1, tiled=True)
    gates = jax.nn.sigmoid(logits).reshape(3 * HEADS, SEG)
    query = queries.transpose(1, 2, 0)
    longest_query = jnp.max(jnp.sum(jnp.square(query.astype(jnp.float32)), axis=1)).reshape(1)
    near = window_of(place, longest_query, query, previous, packed)
    near, safe = coarse_of(place, longest_query, query, coarse, gates, near)
    out = fine_of(safe, lists, query, received, packed, near, gates)
    return out.reshape(SEG, HEADS, DV)


def solution(mesh):
    split = Mesh(
        mesh.devices.reshape(4, 8, mesh.shape["head"], mesh.shape["seg"]),
        ("ctx_0", "ctx_1", "head", "seg"),
    )
    placed = (
        P(CTX_SEG, "head"),
        P(None, None, "head"),
        P(CTX_SEG, "head", None),
        P(CTX_SEG, "head", None),
        P(CTX_SEG, "head", None),
        P("head", None, None),
        P("head", None, None),
        P(CTX_SEG, "head", None),
    )
    return jax.shard_map(
        on_device, mesh=split, in_specs=placed, out_specs=P(CTX_SEG, "head", None), check_vma=False
    )
```
